512 devices in a mesh: region: 8 (over x, core), dev: 64 (over z, y).
Axes of the slice: x: 4, y: 4, z: 16, core: 2. Of those that a mesh axis runs over, the one named last changes fastest.
Arguments:
- positions: float32 [3, 2048, 128], P(None, ('region', 'dev')), as said below
- charges: float32 [2048, 128], P(('region', 'dev')), may hold values from -3 to 3
- types: int32 [2048, 128], P(('region', 'dev')), may hold values from 0 to 5
- pairs: int32 [2048, 13], P(('region', 'dev')), may hold values from -1 to 2047, as said below
- owner_map: int32 [2048], replicated, may hold values from 0 to 2047, as said below
Outputs:
- born_radius: float32 [2048, 128], P(('region', 'dev'))
- energy: float32 [2048, 128], P(('region', 'dev'))
- forces: float32 [3, 2048, 128], P(None, ('region', 'dev'))
- born_grad: float32 [2048, 128], P(('region', 'dev'))
The draws below stay inside these ranges and needn't reach their ends.
Inputs may be any that keep to these rules, and one draw needn't show every extreme that they name: `pairs`: row g lists cells next to block g's cell; -1 marks an empty slot. The block that owner_map gives for a listed cell differs from g and lies in g's region (blocks r * 256 to (r + 1) * 256 - 1) or in the next region. No pair of blocks is listed twice, in either order. `owner_map`: for each region r, a permutation of the cells r * 256 to (r + 1) * 256 - 1 onto the blocks with the same ids. `positions`: any two atoms are 1.5 or more apart.
All inputs are finite; a program needn't handle non-finite values.
Results may differ from the reference program's by a relative error of at most 0.0003.
Values sent between devices are 32-bit elements; how exact they have to be, the bound alone decides.
A program may use at most 64 MiB of HBM per device.

```python
import jax
import jax.numpy as jnp
import numpy as np
from jax import lax

BLK_DEV = 4
LAT_X = 4
LAT_Y = 4
LAT_Z = 8
NTYPES = 6
GRID_Y = 4
ATOMS_BLK = 128
GRID_Z = 16
BLOCKS = 2048
N_REGION = 8
N_DEV = 64


shell_offsets = np.array([[1, -1, -1], [1, -1, 0], [1, -1, 1], [1, 0, -1], [1, 0, 0], [1, 0, 1], [1, 1, -1], [1, 1, 0], [1, 1, 1], [0, 1, -1], [0, 1, 0], [0, 1, 1], [0, 0, 1]], dtype=np.int32)


lattice_spacing = 3.0


def permute_region(sub_key):
    return jax.random.permutation(sub_key, N_DEV * BLK_DEV).astype(jnp.int32)


def layout(key):
    base_key = jax.random.fold_in(key, 4242)
    region_blocks = N_DEV * BLK_DEV
    permuted = jax.vmap(permute_region)(jax.random.split(base_key, N_REGION))
    region_start = (jnp.arange(N_REGION, dtype=jnp.int32) * region_blocks)[:, None]
    owner_map = (permuted + region_start).reshape(-1)
    cell_count = owner_map.shape[0]
    block_cell = jnp.zeros((cell_count,), jnp.int32).at[owner_map].set(jnp.arange(cell_count, dtype=jnp.int32))
    return (owner_map, block_cell)


def cell_coords(cell_ids):
    region_blocks = N_DEV * BLK_DEV
    region_ids = cell_ids // region_blocks
    local_ids = cell_ids % region_blocks
    cell_x = region_ids * BLK_DEV + local_ids // (GRID_Y * GRID_Z)
    cell_y = local_ids // GRID_Z % GRID_Y
    cell_z = local_ids % GRID_Z
    return (cell_x, cell_y, cell_z)


def cell_number(cell_x, cell_y, cell_z):
    region_ids = cell_x // BLK_DEV
    local_ids = cell_x % BLK_DEV * GRID_Y * GRID_Z + cell_y * GRID_Z + cell_z
    return region_ids * (N_DEV * BLK_DEV) + local_ids


def draw_owner_map(key, part):
    owner_map, block_cell = layout(key)
    return owner_map


def draw_pairs(key, part):
    owner_map, block_cell = layout(key)
    cell_x, cell_y, cell_z = cell_coords(block_cell)
    shift_table = jnp.asarray(shell_offsets, jnp.int32)
    near_x = cell_x[:, None] + shift_table[None, :, 0]
    near_y = cell_y[:, None] + shift_table[None, :, 1]
    near_z = cell_z[:, None] + shift_table[None, :, 2]
    inside = (near_x < N_REGION * BLK_DEV) & (near_y >= 0) & (near_y < GRID_Y) & (near_z >= 0) & (near_z < GRID_Z)
    near_id = cell_number(jnp.minimum(near_x, N_REGION * BLK_DEV - 1), jnp.clip(near_y, 0, GRID_Y - 1), jnp.clip(near_z, 0, GRID_Z - 1))
    return jnp.where(inside, near_id, -1).astype(jnp.int32)


def draw_positions(key, part):
    owner_map, block_cell = layout(key)
    cell_x, cell_y, cell_z = cell_coords(block_cell)
    atom_ids = jnp.arange(ATOMS_BLK, dtype=jnp.int32)
    lat_x = atom_ids // (LAT_Y * LAT_Z)
    lat_y = atom_ids // LAT_Z % LAT_Y
    lat_z = atom_ids % LAT_Z
    coord_x = (cell_x[:, None] * LAT_X + lat_x[None]).astype(jnp.float32) + 0.5
    coord_y = (cell_y[:, None] * LAT_Y + lat_y[None]).astype(jnp.float32) + 0.5
    coord_z = (cell_z[:, None] * LAT_Z + lat_z[None]).astype(jnp.float32) + 0.5
    lattice = jnp.stack([coord_x, coord_y, coord_z]) * lattice_spacing
    noise_key = jax.random.fold_in(key, 977)
    uniform_draw = jax.random.uniform(noise_key, lattice.shape, jnp.float32, -1.0, 1.0)
    jitter = uniform_draw
    return lattice + 0.25 * lattice_spacing * jitter


def set_ends(drawn, key, least, high):
    longest = drawn.shape.index(max(drawn.shape))
    spots = []
    for shift in (0, 1):
        where = [jax.random.randint(jax.random.fold_in(key, axis), (), 0, length) for axis, length in enumerate(drawn.shape)]
        where[longest] = (where[longest] + shift) % drawn.shape[longest]
        spots.append(tuple(where))
    return drawn.at[spots[0]].set(least).at[spots[1]].set(high)


def block_scale(own_key, dims, shards, smallest, top_value):
    def one(position, blocks):
        draws = jax.random.uniform(jax.random.fold_in(jax.random.fold_in(own_key, 6), position), (blocks,), jnp.float32, smallest / len(shards), top_value / len(shards))
        return jnp.repeat(jnp.exp(draws), dims[position] // blocks).reshape((-1,) + (1,) * (len(dims) - position - 1))

    gain = one(*shards[0])
    for cut in shards[1:]:
        gain = gain * one(*cut)
    return gain


def scatter_about(key, dims, spread, bound, shards=(), kind=jnp.bfloat16):
    entries = spread * jax.random.normal(key, dims, jnp.float32)
    if shards:
        entries = entries * block_scale(key, dims, shards, -0.22, 0.18)
    return jnp.clip(entries, -bound, bound).astype(kind)


def setup_inputs(seed: int = 0) -> dict:
    key_of = jax.random.split(jax.random.key(seed), 6)
    return {
        "positions": draw_positions(jax.random.fold_in(key_of[5], 71), 0),
        "charges": scatter_about(key_of[1], (BLOCKS, ATOMS_BLK), 0.6, 3.0, ((0, 512),), jnp.float32),
        "types": set_ends(jax.random.randint(key_of[2], (BLOCKS, ATOMS_BLK), 0, NTYPES), jax.random.fold_in(key_of[2], 1), 0, NTYPES - 1).astype(jnp.int32),
        "pairs": draw_pairs(jax.random.fold_in(key_of[5], 71), 0),
        "owner_map": draw_owner_map(jax.random.fold_in(key_of[5], 71), 0),
    }


type_radii = (1.2, 1.7, 1.55, 1.52, 1.85, 1.8)
type_scales = (0.85, 0.72, 0.79, 0.85, 0.86, 0.96)
radius_offset = 0.09
born_alpha = 1.0
born_beta = 0.8
born_gamma = 4.85
solvent_tau = 1.0 - 1.0 / 78.5

def lookup_types(types):
    shape_tail = (-1,) + (1,) * types.ndim
    type_ids = jnp.arange(len(type_radii), dtype=jnp.int32).reshape(shape_tail)
    one_hot = (types[None] == type_ids).astype(jnp.float32)
    radii_table = jnp.asarray(type_radii, jnp.float32).reshape(shape_tail)
    scale_table = jnp.asarray(type_scales, jnp.float32).reshape(shape_tail)
    intrinsic = lax.optimization_barrier(jnp.sum(one_hot * radii_table, axis=0))
    offset_rho = intrinsic - radius_offset
    scaled_rho = lax.optimization_barrier(jnp.sum(one_hot * scale_table, axis=0)) * offset_rho
    return (intrinsic, offset_rho, scaled_rho)

def descreen(distance, rho_self, scaled_other):
    high_edge = distance + scaled_other
    low_edge = jnp.maximum(rho_self, jnp.abs(distance - scaled_other))
    inv_low = 1.0 / low_edge
    inv_high = 1.0 / high_edge
    inv_dist = 1.0 / distance
    integral = inv_low - inv_high + 0.25 * distance * (inv_high * inv_high - inv_low * inv_low) + 0.5 * inv_dist * jnp.log(low_edge * inv_high) + 0.25 * scaled_other * scaled_other * inv_dist * (inv_low * inv_low - inv_high * inv_high)
    inner_term = jnp.where(rho_self < scaled_other - distance, 2.0 * (1.0 / rho_self - inv_low), 0.0)
    return jnp.where(high_edge > rho_self, 0.5 * (integral + inner_term), 0.0)

def masked_sum(values, keep_mask, reduce_axes):
    return lax.optimization_barrier(jnp.sum(jnp.where(keep_mask, values, 0.0), axis=reduce_axes))

def pair_geometry(home_block, partner_fields, usable):
    slot_count = partner_fields.shape[1]
    atom_count = home_block.shape[-1]
    separation = home_block[:3, None, :, None] - partner_fields[:3, :, None, :]
    squared = lax.optimization_barrier(jnp.sum(separation * separation, axis=0))
    slot_ids = jnp.arange(slot_count, dtype=jnp.int32)[:, None, None]
    atom_ids = jnp.arange(atom_count, dtype=jnp.int32)
    diagonal = (slot_ids == 0) & (atom_ids[:, None] == atom_ids[None, :])[None]
    home_mask = usable[:, None, None] & jnp.logical_not(diagonal)
    partner_mask = home_mask & (slot_ids > 0)
    distance = jnp.sqrt(jnp.where(home_mask, squared, 1.0))
    return (separation, distance, home_mask, partner_mask)

def descreen_tile(home_block, partner_fields, usable):
    separation, distance, home_mask, partner_mask = pair_geometry(home_block, partner_fields, usable)
    home_term = descreen(distance, home_block[3][None, :, None], partner_fields[4][:, None, :])
    partner_term = descreen(distance, partner_fields[3][:, None, :], home_block[4][None, :, None])
    return (masked_sum(home_term, home_mask, (0, 2))[None], masked_sum(partner_term, partner_mask, 1)[None])

def energy_tile(home_block, partner_fields, usable):
    separation, distance, home_mask, partner_mask = pair_geometry(home_block, partner_fields, usable)
    charge_prod = solvent_tau * home_block[3][None, :, None] * partner_fields[3][:, None, :]
    radius_home = home_block[4][None, :, None]
    radius_partner = partner_fields[4][:, None, :]
    radius_prod = radius_home * radius_partner
    squared = distance * distance
    exponent_arg = squared / (4.0 * radius_prod)
    damped = jnp.exp(-exponent_arg)
    denom_sq = squared + radius_prod * damped
    denom_root = jnp.sqrt(denom_sq)
    inv_cube = 1.0 / (denom_root * denom_sq)
    pair_energy = -0.5 * charge_prod / denom_root
    pull_coef = -charge_prod * (1.0 - 0.25 * damped) * inv_cube
    grad_common = 0.5 * charge_prod * damped * (1.0 + exponent_arg) * inv_cube
    home_sum = jnp.stack([masked_sum(pull_coef * separation[0], home_mask, (0, 2)), masked_sum(pull_coef * separation[1], home_mask, (0, 2)), masked_sum(pull_coef * separation[2], home_mask, (0, 2)), masked_sum(pair_energy, home_mask, (0, 2)), masked_sum(grad_common * radius_partner, home_mask, (0, 2))])
    other_sum = jnp.stack([masked_sum(-pull_coef * separation[0], partner_mask, 1), masked_sum(-pull_coef * separation[1], partner_mask, 1), masked_sum(-pull_coef * separation[2], partner_mask, 1), masked_sum(pair_energy, partner_mask, 1), masked_sum(grad_common * radius_home, partner_mask, 1)])
    return (home_sum, other_sum)

def sweep(fields, partner_ids, live_slot, tile_fn, field_count):
    block_count = fields.shape[1]
    first_ok = jnp.zeros((1,), jnp.int32) == 0

    def visit(totals, block_index):
        home_block = jnp.take(fields, block_index, axis=1)
        targets = jnp.take(partner_ids, block_index, axis=0)
        usable = jnp.concatenate([first_ok, jnp.take(live_slot, block_index, axis=0)])
        partner_fields = jnp.concatenate([home_block[:, None], jnp.take(fields, targets, axis=1)], axis=1)
        home_sum, other_sum = tile_fn(home_block, partner_fields, usable)
        totals = totals.at[:, block_index].add(home_sum)
        totals = totals.at[:, targets].add(other_sum[:, 1:])
        return (totals, None)
    initial = jnp.zeros((field_count, block_count, fields.shape[2]), jnp.float32)
    totals, unused = lax.scan(visit, initial, jnp.arange(block_count, dtype=jnp.int32))
    return totals

def reference(positions, charges, types, pairs, owner_map):
    intrinsic, offset_rho, scaled_rho = lookup_types(types)
    live_slot = pairs >= 0
    partner_ids = owner_map[jnp.maximum(pairs, 0)]
    first_fields = jnp.concatenate([positions, offset_rho[None], scaled_rho[None]], axis=0)
    descreen_sum = sweep(first_fields, partner_ids, live_slot, descreen_tile, 1)[0]
    psi_value = descreen_sum * offset_rho
    shaped = born_alpha * psi_value - born_beta * psi_value * psi_value + born_gamma * psi_value * psi_value * psi_value
    born_radius = 1.0 / (1.0 / offset_rho - jnp.tanh(shaped) / intrinsic)
    second = jnp.concatenate([positions, charges[None], born_radius[None]], axis=0)
    totals = sweep(second, partner_ids, live_slot, energy_tile, 5)
    charge_sq = solvent_tau * charges * charges
    energy = totals[3] - 0.5 * charge_sq / born_radius
    born_grad = totals[4] + 0.5 * charge_sq / (born_radius * born_radius)
    return (born_radius, energy, totals[:3], born_grad)
```

```python
import functools
import math

import jax
import jax.numpy as jnp
from jax import lax
from jax.experimental import pallas as pl
from jax.experimental.pallas import tpu as pltpu
from jax.sharding import PartitionSpec as P

type_radii = (1.2, 1.7, 1.55, 1.52, 1.85, 1.8)
type_scales = (0.85, 0.72, 0.79, 0.85, 0.86, 0.96)
radius_offset = 0.09
born_alpha = 1.0
born_beta = 0.8
born_gamma = 4.85
solvent_tau = 1.0 - 1.0 / 78.5

MESH = pl.DeviceIdType.MESH
NREG = 8
NZ = 16
NY = 4
NDEV = NZ * NY
BLK = 4
SLOTS = 13
ATOMS = 128
ROWS1 = 24
ROWS2 = 8
REGION_BLOCKS = NDEV * BLK
REV = 32
LIST = 64
F32 = jnp.float32
I32 = jnp.int32
HIGH = lax.Precision.HIGHEST
NT = (((1,), (1,)), ((), ()))


def table(types, values):
    out = jnp.full(types.shape, values[0], F32)
    for i in range(1, len(values)):
        out = jnp.where(types == i, F32(values[i]), out)
    return out


def pack_kernel(pairs, pos, types, out):
    for f in range(3):
        out[4 * f : 4 * f + 4, :] = pos[f]
    kinds = types[...]
    rho = table(kinds, type_radii) - radius_offset
    out[12:16, :] = rho
    out[16:20, :] = table(kinds, type_scales) * rho
    lane = lax.broadcasted_iota(I32, (1, ATOMS), 1)
    row = jnp.full((1, ATOMS), -1, I32)
    for b in range(BLK):
        for k in range(SLOTS):
            row = jnp.where(lane == b * SLOTS + k, pairs[b, k], row)
    out[20:21, :] = row.astype(F32)
    out[21:24, :] = jnp.zeros((3, ATOMS), F32)


def pack(positions, types, pairs):
    return pl.pallas_call(
        pack_kernel,
        out_shape=jax.ShapeDtypeStruct((ROWS1, ATOMS), F32),
        in_specs=[
            pl.BlockSpec(memory_space=pltpu.SMEM),
            pl.BlockSpec(memory_space=pltpu.VMEM),
            pl.BlockSpec(memory_space=pltpu.VMEM),
        ],
        out_specs=pl.BlockSpec(memory_space=pltpu.VMEM),
        name="pack",
    )(pairs, positions, types)


def gather_kernel(x, out, local, ysend, yrecv, zsend, zrecv, fsend, frecv):
    r = lax.axis_index("region")
    d = lax.axis_index("dev")
    z = d // NY
    y = d % NY
    odd = r % 2
    sibling = r + 1 - 2 * odd
    beside = (r + 2 * odd - 1 + NREG) % NREG
    up = (z + 1) % NZ
    down = (z + NZ - 1) % NZ

    peers = [(r, z * NY + (y + k) % NY) for k in range(1, NY)]
    peers += [(r, up * NY + y), (r, down * NY + y), (sibling, d), (beside, d)]
    barrier = pltpu.get_barrier_semaphore()
    for peer in peers:
        pl.semaphore_signal(barrier, inc=1, device_id=peer, device_id_type=MESH)
    own = pltpu.make_async_copy(x, out.at[d], local)
    own.start()
    pl.semaphore_wait(barrier, len(peers))

    sends = []

    def send(src, dst, ssem, rsem, to):
        copy = pltpu.make_async_remote_copy(
            src_ref=src, dst_ref=dst, send_sem=ssem, recv_sem=rsem, device_id=to, device_id_type=MESH
        )
        copy.start()
        sends.append(copy)

    def wait_for(dst, rsem):
        pltpu.make_async_remote_copy(
            src_ref=dst, dst_ref=dst, send_sem=rsem, recv_sem=rsem, device_id=(sibling, d), device_id_type=MESH
        ).wait_recv()

    def column(slot, zz):
        return out.at[pl.ds(slot * NDEV + zz * NY, NY)]

    for k in range(1, NY):
        send(x, out.at[d], ysend.at[k - 1], yrecv.at[k - 1], (r, z * NY + (y + k) % NY))
    own.wait()
    for k in range(1, NY):
        wait_for(out.at[z * NY + (y + NY - k) % NY], yrecv.at[k - 1])

    def forward(zz, n):
        send(column(0, zz), column(2, zz), fsend.at[1, n], frecv.at[1, n], (beside, d))
        send(column(0, zz), column(1, zz), fsend.at[0, n], frecv.at[0, n], (sibling, d))

    half = NZ // 2
    for s in range(1, half + 1):
        behind = (z + NZ - (s - 1)) % NZ
        ahead = (z + (s - 1)) % NZ
        send(column(0, behind), column(0, behind), zsend.at[0, s - 1], zrecv.at[0, s - 1], (r, up * NY + y))
        if s < half:
            send(column(0, ahead), column(0, ahead), zsend.at[1, s - 1], zrecv.at[1, s - 1], (r, down * NY + y))
        forward(behind, s - 1)
        if s > 1:
            forward(ahead, half + s - 1)
        wait_for(column(0, (z + NZ - s) % NZ), zrecv.at[0, s - 1])
        if s < half:
            wait_for(column(0, (z + s) % NZ), zrecv.at[1, s - 1])
    forward((z + half) % NZ, half)

    for n in range(NZ):
        zz = (z + NZ - n) % NZ if n <= half else (z + n - half) % NZ
        wait_for(column(1, zz), frecv.at[0, n])
        wait_for(column(2, zz), frecv.at[1, n])
    for copy in sends:
        copy.wait_send()


def gather(payload, rows, ident):
    dma = pltpu.SemaphoreType.DMA
    return pl.pallas_call(
        gather_kernel,
        out_shape=jax.ShapeDtypeStruct((3 * NDEV, rows, ATOMS), F32),
        in_specs=[pl.BlockSpec(memory_space=pltpu.VMEM)],
        out_specs=pl.BlockSpec(memory_space=pltpu.VMEM),
        scratch_shapes=[
            dma,
            dma((NY - 1,)),
            dma((NY - 1,)),
            dma((2, NZ // 2)),
            dma((2, NZ // 2)),
            dma((2, NZ)),
            dma((2, NZ)),
        ],
        compiler_params=pltpu.CompilerParams(collective_id=ident, has_side_effects=True),
        name="gather%d" % ident,
    )(payload)


def ids_here():
    return lax.axis_index("region"), lax.axis_index("dev")


def spread(columns, ref):
    turned = jnp.transpose(columns)
    for f in range(ref.shape[0]):
        ref[f] = jnp.broadcast_to(turned[:, f : f + 1], (ATOMS, ATOMS))


def row_sums(values):
    return lax.dot_general(jnp.ones((8, ATOMS), F32), values, NT, precision=HIGH, preferred_element_type=F32)[0:1]


def h_term(r2, a, ia2, s):
    ir = lax.rsqrt(r2)
    r = r2 * ir
    upper = r + s
    gap = r - s
    lower = jnp.maximum(a, jnp.abs(gap))
    il = 1.0 / lower
    iu = 1.0 / upper
    dif = il - iu
    tot = il + iu
    bent = 0.25 * (s * s * ir - r)
    value = dif + dif * tot * bent + (0.5 * math.log(2.0)) * ir * jnp.log2(lower * iu)
    value = value + jnp.where(gap < -a, ia2 - (il + il), 0.0)
    return jnp.where(upper > a, value, 0.0)


def find_partners(r, d, pairs, owners_s, owners, fields, lst, cnt, found, found_s, sem):
    odd = r % 2
    previous = 2 - odd
    base = r * REGION_BLOCKS + d * BLK
    ids = lax.broadcasted_iota(I32, (16, ATOMS), 0) * ATOMS + lax.broadcasted_iota(I32, (16, ATOMS), 1)
    held = owners[...]
    listed = jnp.concatenate(
        [
            fields[pl.ds(20, NDEV, stride=ROWS1), :],
            fields[pl.ds(previous * NDEV * ROWS1 + 20, NDEV, stride=ROWS1), :],
        ],
        axis=0,
    )
    sub = lax.broadcasted_iota(I32, (16, ATOMS), 0)
    lane = lax.broadcasted_iota(I32, (16, ATOMS), 1)
    hits = jnp.zeros((16, ATOMS), F32)
    for b in range(BLK):
        cell = jnp.sum(jnp.where(held == base + b, ids, 0).astype(F32))
        match = (listed == cell).astype(F32)
        pick = ((sub // BLK == b) & (lane // SLOTS == sub % BLK)).astype(F32)
        hits = hits + lax.dot_general(pick, match, NT, preferred_element_type=F32)
    row = lax.broadcasted_iota(I32, (ATOMS, ATOMS), 0)
    col = lax.broadcasted_iota(I32, (ATOMS, ATOMS), 1)
    prefix = (row <= col).astype(F32)
    s0 = lax.broadcasted_iota(I32, (16, 16), 0)
    s1 = lax.broadcasted_iota(I32, (16, 16), 1)
    before = ((s0 // BLK == s1 // BLK) & (s1 < s0)).astype(F32)
    rank = jnp.dot(hits, prefix, preferred_element_type=F32)
    earlier = jnp.dot(before, hits, preferred_element_type=F32)
    rank = rank + jnp.dot(earlier, jnp.ones((ATOMS, ATOMS), F32), preferred_element_type=F32)
    rank = jnp.where(hits > 0.5, rank, 0.0)
    wanted = (lax.broadcasted_iota(I32, (REV, ATOMS), 0) + 1).astype(F32)
    slot_dev = lax.broadcasted_iota(I32, (1, ATOMS), 1)
    slot_dev = jnp.where(slot_dev < NDEV, slot_dev, slot_dev + (previous - 1) * NDEV)
    picked = []
    for b in range(BLK):
        total = jnp.zeros((REV, ATOMS), F32)
        for o in range(BLK):
            code = (slot_dev * BLK + o + 1).astype(F32)
            total = total + jnp.where(rank[b * BLK + o : b * BLK + o + 1] == wanted, code, 0.0)
        picked.append(total)
    picked = jnp.concatenate(picked, axis=0)
    codes = lax.dot_general(jnp.ones((8, ATOMS), F32), picked, NT, precision=HIGH, preferred_element_type=F32)
    found[...] = (codes + 0.5).astype(I32)
    copy = pltpu.make_async_copy(found, found_s, sem)
    copy.start()
    for b in range(BLK):

        def listing(k, n, b=b):
            cell = pairs[b, k]
            partner = owners_s[jnp.maximum(cell, 0)]
            region = partner // REGION_BLOCKS
            slot = jnp.where(region == r, 0, jnp.where(region == r + 1 - 2 * odd, 1, 2))
            lst[b, n] = slot * REGION_BLOCKS + partner % REGION_BLOCKS
            return n + (cell >= 0).astype(I32)

        cnt[b] = lax.fori_loop(0, SLOTS, listing, jnp.int32(0), unroll=True)
    copy.wait()
    for b in range(BLK):

        def reverse(k, n, b=b):
            code = found_s[0, b * REV + k]
            lst[b, n] = code - 1
            return n + (code > 0).astype(I32)

        cnt[b] = lax.fori_loop(0, REV, reverse, cnt[b], unroll=8)


CHUNK1 = 64
CHUNK2 = 32


def fetch(ref, start):
    return ref[pl.ds(start, 1), :]


def descreen_kernel(
    where, pairs, owners_s, owners, types, charges, fields, out, lst, cnt, home, acc, found, found_s, sem
):
    r, d = where()
    find_partners(r, d, pairs, owners_s, owners, fields, lst, cnt, found, found_s, sem)
    sums = []
    for b in range(BLK):
        own = d * ROWS1 + b
        rho_row = fetch(fields, own + 12)
        rows = [fetch(fields, own), fetch(fields, own + 4), fetch(fields, own + 8), rho_row, 2.0 / rho_row]
        spread(jnp.concatenate(rows + [jnp.zeros((3, ATOMS), F32)], axis=0), home)

        def chunk(c, carry, b=b, own=own):
            span = pl.ds(pl.multiple_of(c * CHUNK1, CHUNK1), CHUNK1)
            hx, hy, hz, ha, hi = (home[f, span, :] for f in range(5))

            def tile(start, mask=None):
                dx = hx - fetch(fields, start)
                dy = hy - fetch(fields, start + 4)
                dz = hz - fetch(fields, start + 8)
                r2 = dx * dx + dy * dy + dz * dz
                if mask is not None:
                    r2 = jnp.where(mask, 1.0, r2)
                return h_term(r2, ha, hi, fetch(fields, start + 16))

            diagonal = lax.broadcasted_iota(I32, (CHUNK1, ATOMS), 1) == (
                lax.broadcasted_iota(I32, (CHUNK1, ATOMS), 0) + c * CHUNK1
            )
            total = jnp.where(diagonal, 0.0, tile(own, diagonal))

            def step(n, total):
                e = lst[b, n]
                return total + tile((e // BLK) * ROWS1 + e % BLK)

            acc[span, :] = lax.fori_loop(0, cnt[b], step, total)
            return carry

        lax.fori_loop(0, ATOMS // CHUNK1, chunk, 0)
        sums.append(row_sums(acc[...]))
    descreen = 0.5 * jnp.concatenate(sums, axis=0)
    rho0 = table(types[...], type_radii)
    rho = rho0 - radius_offset
    psi = descreen * rho
    shaped = born_alpha * psi - born_beta * psi * psi + born_gamma * psi * psi * psi
    out[0:4, :] = 1.0 / (1.0 / rho - jnp.tanh(shaped) / rho0)
    out[4:8, :] = charges[...]


def descreen_stage(where, pairs, owner_map, types, charges, fields):
    smem = pl.BlockSpec(memory_space=pltpu.SMEM)
    vmem = pl.BlockSpec(memory_space=pltpu.VMEM)
    return pl.pallas_call(
        functools.partial(descreen_kernel, where),
        out_shape=(
            jax.ShapeDtypeStruct((ROWS2, ATOMS), F32),
            jax.ShapeDtypeStruct((BLK, LIST), I32),
            jax.ShapeDtypeStruct((BLK,), I32),
        ),
        in_specs=[smem, smem, vmem, vmem, vmem, vmem],
        out_specs=(vmem, smem, smem),
        scratch_shapes=[
            pltpu.VMEM((5, ATOMS, ATOMS), F32),
            pltpu.VMEM((ATOMS, ATOMS), F32),
            pltpu.VMEM((8, ATOMS), I32),
            pltpu.SMEM((8, ATOMS), I32),
            pltpu.SemaphoreType.DMA,
        ],
        name="descreen",
    )(pairs, owner_map, owner_map.reshape(16, ATOMS), types, charges, fields.reshape(-1, ATOMS))


def energy_kernel(where, lst, cnt, fields, radii, energy, forces, grad, home, acc):
    r, d = where()
    for b in range(BLK):
        own = d * ROWS1 + b
        own2 = d * ROWS2 + b
        radius = fetch(radii, own2)
        charge = fetch(radii, own2 + 4)
        inverse = 1.0 / radius
        rows = [fetch(fields, own), fetch(fields, own + 4), fetch(fields, own + 8), solvent_tau * charge, radius]
        rows.append((-0.25 * math.log2(math.e)) * inverse)
        spread(jnp.concatenate(rows + [jnp.zeros((2, ATOMS), F32)], axis=0), home)

        def chunk(c, carry, b=b, own=own, own2=own2):
            span = pl.ds(pl.multiple_of(c * CHUNK2, CHUNK2), CHUNK2)
            hx, hy, hz, hq, hr, hd = (home[f, span, :] for f in range(6))

            def tile(start, start2, totals, mask=None):
                dx = hx - fetch(fields, start)
                dy = hy - fetch(fields, start + 4)
                dz = hz - fetch(fields, start + 8)
                radius_j = fetch(radii, start2)
                charge_j = fetch(radii, start2 + 4)
                r2 = dx * dx + dy * dy + dz * dz
                if mask is not None:
                    r2 = jnp.where(mask, 1.0, r2)
                arg = r2 * (hd * (1.0 / radius_j))
                damped = jnp.exp2(arg)
                inv = lax.rsqrt(r2 + hr * radius_j * damped)
                e = hq * charge_j * inv
                if mask is not None:
                    e = jnp.where(mask, 0.0, e)
                e3 = e * (inv * inv)
                e3d = e3 * damped
                pull = e3 - 0.25 * e3d
                g = (e3d * radius_j) * (1.0 - math.log(2.0) * arg)
                fx, fy, fz, te, tg = totals
                return (fx + pull * dx, fy + pull * dy, fz + pull * dz, te + e, tg + g)

            diagonal = lax.broadcasted_iota(I32, (CHUNK2, ATOMS), 1) == (
                lax.broadcasted_iota(I32, (CHUNK2, ATOMS), 0) + c * CHUNK2
            )
            totals = (jnp.zeros((CHUNK2, ATOMS), F32),) * 5
            totals = tile(own, own2, totals, diagonal)

            def step(n, totals):
                e = lst[b, n]
                dev = e // BLK
                blk = e % BLK
                return tile(dev * ROWS1 + blk, dev * ROWS2 + blk, totals)

            totals = lax.fori_loop(0, cnt[b], step, totals)
            for f in range(5):
                acc[f, span, :] = totals[f]
            return carry

        lax.fori_loop(0, ATOMS // CHUNK2, chunk, 0)
        for f in range(3):
            forces[f, b : b + 1, :] = -row_sums(acc[f])
        self_e = solvent_tau * charge * charge
        energy[b : b + 1, :] = -0.5 * row_sums(acc[3]) - 0.5 * self_e * inverse
        grad[b : b + 1, :] = 0.5 * row_sums(acc[4]) + 0.5 * self_e * inverse * inverse


def energy_stage(where, lst, cnt, fields, radii):
    smem = pl.BlockSpec(memory_space=pltpu.SMEM)
    vmem = pl.BlockSpec(memory_space=pltpu.VMEM)
    return pl.pallas_call(
        functools.partial(energy_kernel, where),
        out_shape=(
            jax.ShapeDtypeStruct((BLK, ATOMS), F32),
            jax.ShapeDtypeStruct((3, BLK, ATOMS), F32),
            jax.ShapeDtypeStruct((BLK, ATOMS), F32),
        ),
        in_specs=[smem, smem, vmem, vmem],
        out_specs=(vmem, vmem, vmem),
        scratch_shapes=[pltpu.VMEM((6, ATOMS, ATOMS), F32), pltpu.VMEM((5, ATOMS, ATOMS), F32)],
        name="energy",
    )(lst, cnt, fields.reshape(-1, ATOMS), radii.reshape(-1, ATOMS))


def shards(positions, charges, types, pairs, owner_map):
    fields = gather(pack(positions, types, pairs), ROWS1, 0)
    mine, lst, cnt = descreen_stage(ids_here, pairs, owner_map, types, charges, fields)
    radii = gather(mine, ROWS2, 1)
    energy, forces, grad = energy_stage(ids_here, lst, cnt, fields, radii)
    return (mine[:BLK], energy, forces, grad)


def solution(mesh):
    placed = (
        P(None, ("region", "dev"), None),
        P(("region", "dev"), None),
        P(("region", "dev"), None),
        P(("region", "dev"), None),
        P(),
    )
    return jax.shard_map(
        shards,
        mesh=mesh,
        in_specs=placed,
        out_specs=(
            P(("region", "dev"), None),
            P(("region", "dev"), None),
            P(None, ("region", "dev"), None),
            P(("region", "dev"), None),
        ),
        check_vma=False,
    )
```

```python
import functools
import math

import jax
import jax.numpy as jnp
from jax import lax
from jax.experimental import pallas as pl
from jax.experimental.pallas import tpu as pltpu
from jax.sharding import PartitionSpec as P

type_radii = (1.2, 1.7, 1.55, 1.52, 1.85, 1.8)
type_scales = (0.85, 0.72, 0.79, 0.85, 0.86, 0.96)
radius_offset = 0.09
born_alpha = 1.0
born_beta = 0.8
born_gamma = 4.85
solvent_tau = 1.0 - 1.0 / 78.5

MESH = pl.DeviceIdType.MESH
NREG = 8
NZ = 16
NY = 4
NDEV = NZ * NY
BLK = 4
SLOTS = 13
ATOMS = 128
ROWS1 = 17
ROWS2 = 8
REGION_BLOCKS = NDEV * BLK
REV = 32
LIST = 64
HALF = NZ // 2
REACH = 4
PIECES = ((4, 13), (0, 4), (13, 16))
F32 = jnp.float32
I32 = jnp.int32
HIGH = lax.Precision.HIGHEST
NT = (((1,), (1,)), ((), ()))


def table(types, values):
    out = jnp.full(types.shape, values[0], F32)
    for i in range(1, len(values)):
        out = jnp.where(types == i, F32(values[i]), out)
    return out


def gather_body(fill, x, out, local, zsend, zrecv, ysend, yrecv, fsend, frecv):
    r = lax.axis_index("region")
    d = lax.axis_index("dev")
    z = d // NY
    y = d % NY
    odd = r % 2
    sibling = (r + 1 - 2 * odd, d)
    beside = ((r + 2 * odd - 1 + NREG) % NREG, d)

    def zpeer(k):
        return (r, (z + k + NZ) % NZ * NY + y)

    hops = sorted((k for k in range(-REACH, REACH + 1) if k), key=abs)
    ypeers = [(r, z * NY + (y + k) % NY) for k in range(1, NY)]
    everyone = [zpeer(k) for k in hops] + ypeers + [sibling, beside]
    barrier = pltpu.get_barrier_semaphore()
    for peer in everyone:
        pl.semaphore_signal(barrier, inc=1, device_id=peer, device_id_type=MESH)
    fill()
    pl.semaphore_wait(barrier, len(everyone))
    mine = out.at[0, y, HALF]
    own = pltpu.make_async_copy(x, mine, local)
    own.start()
    own.wait()
    sends = []

    def send(src, dst, ssem, rsem, to):
        copy = pltpu.make_async_remote_copy(
            src_ref=src, dst_ref=dst, send_sem=ssem, recv_sem=rsem, device_id=to, device_id_type=MESH
        )
        copy.start()
        sends.append(copy)

    def wait_for(dst, rsem):
        pltpu.make_async_remote_copy(
            src_ref=dst, dst_ref=dst, send_sem=rsem, recv_sem=rsem, device_id=sibling, device_id_type=MESH
        ).wait_recv()

    def part(slot, yy, a, b):
        return out.at[slot, yy, pl.ds(a, b - a)]

    for n, k in enumerate(hops):
        send(mine, out.at[0, y, HALF - k], zsend.at[n], zrecv.at[HALF - k], zpeer(k))

    def forward(yy, k, p):
        span = PIECES[p]
        send(part(0, yy, *span), part(2, yy, *span), fsend.at[1, k, p], frecv.at[1, k, p], beside)
        send(part(0, yy, *span), part(1, yy, *span), fsend.at[0, k, p], frecv.at[0, k, p], sibling)

    low, high = HALF - REACH, HALF + REACH + 1
    for p, span in enumerate(PIECES):
        if p == 0:
            for k in hops:
                wait_for(out.at[0, y, HALF + k], zrecv.at[HALF + k])
            send(part(0, y, low, HALF), part(0, y, 0, low), zsend.at[2 * REACH], zrecv.at[0], zpeer(REACH))
            send(
                part(0, y, HALF + 1, HALF + REACH),
                part(0, y, high, NZ),
                zsend.at[2 * REACH + 1],
                zrecv.at[high],
                zpeer(-REACH),
            )
        else:
            wait_for(part(0, y, *span), zrecv.at[span[0]])
        for k in (2, 1, 3):
            send(part(0, y, *span), part(0, y, *span), ysend.at[k - 1, p], yrecv.at[k - 1, p], ypeers[k - 1])
        forward(y, 0, p)
        for q in [p - 1] * (p > 0) + [p] * (p == len(PIECES) - 1):
            for k in (1, 3, 2):
                yy = (y + NY - k) % NY
                wait_for(part(0, yy, *PIECES[q]), yrecv.at[k - 1, q])
                forward(yy, k, q)
    for p, span in enumerate(PIECES):
        for k in range(NY):
            yy = (y + NY - k) % NY
            wait_for(part(1, yy, *span), frecv.at[0, k, p])
            wait_for(part(2, yy, *span), frecv.at[1, k, p])
    for copy in sends:
        copy.wait_send()


def gather_scratch():
    dma = pltpu.SemaphoreType.DMA
    parts = len(PIECES)
    return [
        dma,
        dma((NZ,)),
        dma((NZ,)),
        dma((NY - 1, parts)),
        dma((NY - 1, parts)),
        dma((2, NY, parts)),
        dma((2, NY, parts)),
    ]


def fields_kernel(pairs, pos, types, out, x, *sems):
    def fill():
        for b in range(BLK):
            for f in range(3):
                x[4 * f + b, :, :] = pos[f, b : b + 1, :]
            x[12 + b, :, :] = types[b : b + 1, :].astype(F32)
        lane = lax.broadcasted_iota(I32, (1, ATOMS), 1)
        row = jnp.full((1, ATOMS), -1, I32)
        for b in range(BLK):
            for k in range(SLOTS):
                row = jnp.where(lane == b * SLOTS + k, pairs[b, k], row)
        x[16, :, :] = row.astype(F32)

    gather_body(fill, x, out, *sems)


def gather_fields(positions, types, pairs):
    vmem = pl.BlockSpec(memory_space=pltpu.VMEM)
    return pl.pallas_call(
        fields_kernel,
        out_shape=jax.ShapeDtypeStruct((3, NY, NZ, ROWS1, 1, ATOMS), F32),
        in_specs=[pl.BlockSpec(memory_space=pltpu.SMEM), vmem, vmem],
        out_specs=vmem,
        scratch_shapes=[pltpu.VMEM((ROWS1, 1, ATOMS), F32)] + gather_scratch(),
        compiler_params=pltpu.CompilerParams(collective_id=0, has_side_effects=True),
        name="gather_fields",
    )(pairs, positions, types)


def radii_kernel(x, out, *sems):
    gather_body(lambda: None, x, out, *sems)


def gather_radii(payload):
    vmem = pl.BlockSpec(memory_space=pltpu.VMEM)
    return pl.pallas_call(
        radii_kernel,
        out_shape=jax.ShapeDtypeStruct((3, NY, NZ, ROWS2, ATOMS), F32),
        in_specs=[vmem],
        out_specs=vmem,
        scratch_shapes=gather_scratch(),
        compiler_params=pltpu.CompilerParams(collective_id=1, has_side_effects=True),
        name="gather_radii",
    )(payload)


def ids_here():
    return lax.axis_index("region"), lax.axis_index("dev")


def own_place(d):
    return (d & (NY - 1)) * NZ + HALF


def spread(columns, ref):
    turned = jnp.transpose(columns)
    for f in range(ref.shape[0]):
        ref[f] = jnp.broadcast_to(turned[:, f : f + 1], (ATOMS, ATOMS))


def row_sums(values):
    return lax.dot_general(jnp.ones((8, ATOMS), F32), values, NT, precision=HIGH, preferred_element_type=F32)[0:1]


def h_term(r2, a, ia8, s):
    ir = lax.rsqrt(r2)
    r = r2 * ir
    upper = r + s
    gap = s - r
    lower = jnp.maximum(a, jnp.abs(gap))
    il = 1.0 / lower
    iu = 1.0 / upper
    value = (il - iu) * (4.0 + (il + iu) * (s * s * ir - r)) + (ir + ir) * jnp.log(lower * iu)
    value = value + jnp.where(a < gap, ia8 - 8.0 * il, 0.0)
    return jnp.where(upper > a, value, 0.0)


def find_partners(r, d, pairs, owners_s, owners, fields, lst1, lst2, cnt, listed, found, found_s, sem):
    odd = r & 1
    previous = 2 - odd
    base = r * REGION_BLOCKS + d * BLK
    ids = lax.broadcasted_iota(I32, (16, ATOMS), 0) * ATOMS + lax.broadcasted_iota(I32, (16, ATOMS), 1)
    held = owners[...]
    for half, place in enumerate((0, previous * NDEV)):

        def take(n, carry, half=half, place=place):
            listed[pl.ds(half * NDEV + n, 1), :] = fields[(place + n) * ROWS1 + 16]
            return carry

        lax.fori_loop(0, NDEV, take, 0, unroll=16)
    known = listed[...]
    sub = lax.broadcasted_iota(I32, (16, ATOMS), 0)
    lane = lax.broadcasted_iota(I32, (16, ATOMS), 1)
    hits = jnp.zeros((16, ATOMS), F32)
    for b in range(BLK):
        cell = jnp.sum(jnp.where(held == base + b, ids, 0).astype(F32))
        match = (known == cell).astype(F32)
        first = (sub & 3) * SLOTS
        pick = (((sub >> 2) == b) & (lane >= first) & (lane < first + SLOTS)).astype(F32)
        hits = hits + lax.dot_general(pick, match, NT, preferred_element_type=F32)
    row = lax.broadcasted_iota(I32, (ATOMS, ATOMS), 0)
    col = lax.broadcasted_iota(I32, (ATOMS, ATOMS), 1)
    prefix = (row <= col).astype(F32)
    s0 = lax.broadcasted_iota(I32, (16, 16), 0)
    s1 = lax.broadcasted_iota(I32, (16, 16), 1)
    before = (((s0 >> 2) == (s1 >> 2)) & (s1 < s0)).astype(F32)
    rank = jnp.dot(hits, prefix, preferred_element_type=F32)
    earlier = jnp.dot(before, hits, preferred_element_type=F32)
    rank = rank + jnp.dot(earlier, jnp.ones((ATOMS, ATOMS), F32), preferred_element_type=F32)
    rank = jnp.where(hits > 0.5, rank, 0.0)
    wanted = (lax.broadcasted_iota(I32, (REV, ATOMS), 0) + 1).astype(F32)
    place = lax.broadcasted_iota(I32, (1, ATOMS), 1)
    place = jnp.where(place < NDEV, place, place + (previous - 1) * NDEV)
    picked = []
    for b in range(BLK):
        total = jnp.zeros((REV, ATOMS), F32)
        for o in range(BLK):
            code = (place * BLK + o + 1).astype(F32)
            total = total + jnp.where(rank[b * BLK + o : b * BLK + o + 1] == wanted, code, 0.0)
        picked.append(total)
    picked = jnp.concatenate(picked, axis=0)
    codes = lax.dot_general(jnp.ones((8, ATOMS), F32), picked, NT, precision=HIGH, preferred_element_type=F32)
    found[...] = (codes + 0.5).astype(I32)
    copy = pltpu.make_async_copy(found, found_s, sem)
    copy.start()
    here = d >> 2

    def note(b, n, place, block):
        lst1[b, n] = place * ROWS1 + block
        lst2[b, n] = place * ROWS2 + block

    for b in range(BLK):

        def listing(k, n, b=b):
            cell = pairs[b, k]
            partner = owners_s[jnp.maximum(cell, 0)]
            region = partner >> 8
            slot = jnp.where(region == r, 0, jnp.where(region == r + 1 - 2 * odd, 1, 2))
            dev = (partner >> 2) & (NDEV - 1)
            offset = ((dev >> 2) - here + HALF) & (NZ - 1)
            note(b, n, slot * NDEV + (dev & 3) * NZ + offset, partner & 3)
            return n + (cell >= 0).astype(I32)

        cnt[b] = lax.fori_loop(0, SLOTS, listing, jnp.int32(0), unroll=True)
    copy.wait()
    for b in range(BLK):

        def reverse(k, n, b=b):
            code = found_s[0, b * REV + k]
            note(b, n, jnp.maximum(code - 1, 0) >> 2, (code - 1) & 3)
            return n + (code > 0).astype(I32)

        cnt[b] = lax.fori_loop(0, REV, reverse, cnt[b], unroll=8)


GROUP = 64


def groups():
    return [pl.ds(g, GROUP) for g in range(0, ATOMS, GROUP)]


def diagonal(g):
    return lax.broadcasted_iota(I32, (GROUP, ATOMS), 1) == lax.broadcasted_iota(I32, (GROUP, ATOMS), 0) + g.start


def descreen_kernel(
    where, pairs, owners_s, owners, types, charges, fields, out, lst1, lst2, cnt, home, acc, listed, found, found_s, sem
):
    r, d = where()
    find_partners(r, d, pairs, owners_s, owners, fields, lst1, lst2, cnt, listed, found, found_s, sem)
    sums = []
    for b in range(BLK):
        own = own_place(d) * ROWS1 + b
        rho_row = table(types[b : b + 1, :], type_radii) - radius_offset
        rows = [fields[own], fields[own + 4], fields[own + 8], rho_row, 8.0 / rho_row]
        spread(jnp.concatenate(rows + [jnp.zeros((3, ATOMS), F32)], axis=0), home)

        def tile(start, first):
            x, y, z, kind = (fields[start + 4 * f] for f in range(4))
            s = table(kind, type_scales) * (table(kind, type_radii) - radius_offset)
            for g in groups():
                hx, hy, hz, ha, hi = (home[f, g, :] for f in range(5))
                dx = hx - x
                dy = hy - y
                dz = hz - z
                r2 = dx * dx + dy * dy + dz * dz
                if first:
                    mask = diagonal(g)
                    acc[g, :] = jnp.where(mask, 0.0, h_term(jnp.where(mask, 1.0, r2), ha, hi, s))
                else:
                    acc[g, :] += h_term(r2, ha, hi, s)

        tile(own, True)

        def step(n, carry, b=b):
            tile(lst1[b, n], False)
            return carry

        lax.fori_loop(0, cnt[b], step, 0)
        sums.append(row_sums(acc[...]))
    descreen = 0.125 * jnp.concatenate(sums, axis=0)
    rho0 = table(types[...], type_radii)
    rho = rho0 - radius_offset
    psi = descreen * rho
    shaped = born_alpha * psi - born_beta * psi * psi + born_gamma * psi * psi * psi
    out[0:4, :] = 1.0 / (1.0 / rho - jnp.tanh(shaped) / rho0)
    out[4:8, :] = charges[...]


def descreen_stage(where, pairs, owner_map, types, charges, fields):
    smem = pl.BlockSpec(memory_space=pltpu.SMEM)
    vmem = pl.BlockSpec(memory_space=pltpu.VMEM)
    return pl.pallas_call(
        functools.partial(descreen_kernel, where),
        out_shape=(
            jax.ShapeDtypeStruct((ROWS2, ATOMS), F32),
            jax.ShapeDtypeStruct((BLK, LIST), I32),
            jax.ShapeDtypeStruct((BLK, LIST), I32),
            jax.ShapeDtypeStruct((BLK,), I32),
        ),
        in_specs=[smem, smem, vmem, vmem, vmem, vmem],
        out_specs=(vmem, smem, smem, smem),
        scratch_shapes=[
            pltpu.VMEM((5, ATOMS, ATOMS), F32),
            pltpu.VMEM((ATOMS, ATOMS), F32),
            pltpu.VMEM((ATOMS, ATOMS), F32),
            pltpu.VMEM((8, ATOMS), I32),
            pltpu.SMEM((8, ATOMS), I32),
            pltpu.SemaphoreType.DMA,
        ],
        name="descreen",
    )(pairs, owner_map, owner_map.reshape(16, ATOMS), types, charges, fields.reshape(-1, 1, ATOMS))


def energy_kernel(where, lst1, lst2, cnt, fields, radii, energy, forces, grad, home, acc):
    r, d = where()
    for b in range(BLK):
        own = own_place(d) * ROWS1 + b
        own2 = own_place(d) * ROWS2 + b
        radius = radii[pl.ds(own2, 1), :]
        charge = radii[pl.ds(own2 + 4, 1), :]
        inverse = 1.0 / radius
        rows = [fields[own], fields[own + 4], fields[own + 8], solvent_tau * charge, radius]
        rows.append((-0.25 * math.log2(math.e)) * inverse)
        spread(jnp.concatenate(rows + [jnp.zeros((2, ATOMS), F32)], axis=0), home)

        def tile(start, start2, first):
            x, y, z = (fields[start + 4 * f] for f in range(3))
            radius_j = radii[pl.ds(start2, 1), :]
            charge_j = radii[pl.ds(start2 + 4, 1), :]
            inverse_j = 1.0 / radius_j
            for g in groups():
                hx, hy, hz, hq, hr, hd = (home[f, g, :] for f in range(6))
                dx = hx - x
                dy = hy - y
                dz = hz - z
                r2 = dx * dx + dy * dy + dz * dz
                if first:
                    mask = diagonal(g)
                    r2 = jnp.where(mask, 1.0, r2)
                arg = r2 * (hd * inverse_j)
                damped = jnp.exp2(arg)
                inv = lax.rsqrt(r2 + hr * radius_j * damped)
                e = hq * charge_j * inv
                if first:
                    e = jnp.where(mask, 0.0, e)
                e3 = e * (inv * inv)
                e3d = e3 * damped
                pull = e3 - 0.25 * e3d
                terms = (pull * dx, pull * dy, pull * dz, e, (e3d * radius_j) * (1.0 - math.log(2.0) * arg))
                for f in range(5):
                    if first:
                        acc[f, g, :] = terms[f]
                    else:
                        acc[f, g, :] += terms[f]

        tile(own, own2, True)

        def step(n, carry, b=b):
            tile(lst1[b, n], lst2[b, n], False)
            return carry

        lax.fori_loop(0, cnt[b], step, 0)
        for f in range(3):
            forces[f, b : b + 1, :] = -row_sums(acc[f])
        self_e = solvent_tau * charge * charge
        energy[b : b + 1, :] = -0.5 * row_sums(acc[3]) - 0.5 * self_e * inverse
        grad[b : b + 1, :] = 0.5 * row_sums(acc[4]) + 0.5 * self_e * inverse * inverse


def energy_stage(where, lst1, lst2, cnt, fields, radii):
    smem = pl.BlockSpec(memory_space=pltpu.SMEM)
    vmem = pl.BlockSpec(memory_space=pltpu.VMEM)
    return pl.pallas_call(
        functools.partial(energy_kernel, where),
        out_shape=(
            jax.ShapeDtypeStruct((BLK, ATOMS), F32),
            jax.ShapeDtypeStruct((3, BLK, ATOMS), F32),
            jax.ShapeDtypeStruct((BLK, ATOMS), F32),
        ),
        in_specs=[smem, smem, smem, vmem, vmem],
        out_specs=(vmem, vmem, vmem),
        scratch_shapes=[pltpu.VMEM((6, ATOMS, ATOMS), F32), pltpu.VMEM((5, ATOMS, ATOMS), F32)],
        name="energy",
    )(lst1, lst2, cnt, fields.reshape(-1, 1, ATOMS), radii.reshape(-1, ATOMS))


def shards(positions, charges, types, pairs, owner_map):
    fields = gather_fields(positions, types, pairs)
    mine, lst1, lst2, cnt = descreen_stage(ids_here, pairs, owner_map, types, charges, fields)
    radii = gather_radii(mine)
    energy, forces, grad = energy_stage(ids_here, lst1, lst2, cnt, fields, radii)
    return (mine[:BLK], energy, forces, grad)


def solution(mesh):
    placed = (
        P(None, ("region", "dev"), None),
        P(("region", "dev"), None),
        P(("region", "dev"), None),
        P(("region", "dev"), None),
        P(),
    )
    return jax.shard_map(
        shards,
        mesh=mesh,
        in_specs=placed,
        out_specs=(
            P(("region", "dev"), None),
            P(("region", "dev"), None),
            P(None, ("region", "dev"), None),
            P(("region", "dev"), None),
        ),
        check_vma=False,
    )
```

```python
import functools
import math

import jax
import jax.numpy as jnp
import numpy as np
from jax import lax
from jax.experimental import pallas as pl
from jax.experimental.pallas import tpu as pltpu
from jax.sharding import PartitionSpec as P

type_radii = (1.2, 1.7, 1.55, 1.52, 1.85, 1.8)
type_scales = (0.85, 0.72, 0.79, 0.85, 0.86, 0.96)
radius_offset = 0.09
born_alpha = 1.0
born_beta = 0.8
born_gamma = 4.85
solvent_tau = 1.0 - 1.0 / 78.5

MESH = pl.DeviceIdType.MESH
NREG = 8
NZ = 16
NY = 4
NDEV = NZ * NY
BLK = 4
SLOTS = 13
ATOMS = 128
ROWS1 = 17
ROWS2 = 8
REGION_BLOCKS = NDEV * BLK
REV = 32
LIST = 64
HALF = NZ // 2
REACH = 4
PIECES = ((4, 13), (0, 4), (13, 16))
F32 = jnp.float32
I32 = jnp.int32
HIGH = lax.Precision.HIGHEST
NT = (((1,), (1,)), ((), ()))


scaled_values = [float(np.float32(s) * (np.float32(v) - np.float32(radius_offset))) for s, v in zip(type_scales, type_radii)]


def table(types, values):
    out = jnp.full(types.shape, values[0], F32)
    for i in range(1, len(values)):
        out = jnp.where(types == i, F32(values[i]), out)
    return out


TILES = 2 * SLOTS
NOWHERE = -1e30


def far_peers():
    r = lax.axis_index("region")
    d = lax.axis_index("dev")
    z = d // NY
    y = d % NY
    odd = r % 2
    hops = sorted((k for k in range(-REACH, REACH + 1) if k), key=abs)
    along = {k: (r, (z + k + NZ) % NZ * NY + y) for k in hops}
    across = [(r, z * NY + (y + k) % NY) for k in range(1, NY)]
    sibling = (r + 1 - 2 * odd, d)
    beside = ((r + 2 * odd - 1 + NREG) % NREG, d)
    return r, d, y, along, across, sibling, beside


def gather_body(peers, out, zsend, zrecv, ysend, yrecv, fsend, frecv, idle):
    r, d, y, along, across, sibling, beside = peers
    sends = []

    def send(src, dst, ssem, rsem, to):
        copy = pltpu.make_async_remote_copy(
            src_ref=src, dst_ref=dst, send_sem=ssem, recv_sem=rsem, device_id=to, device_id_type=MESH
        )
        copy.start()
        sends.append(copy)

    def wait_for(dst, rsem):
        pltpu.make_async_remote_copy(
            src_ref=dst, dst_ref=dst, send_sem=rsem, recv_sem=rsem, device_id=sibling, device_id_type=MESH
        ).wait_recv()

    def part(slot, yy, a, b):
        return out.at[pl.ds((slot * NY + yy) * NZ + a, b - a)]

    def single(o):
        return part(0, y, o, o + 1)

    for n, k in enumerate(along):
        send(single(HALF), single(HALF - k), zsend.at[n], zrecv.at[HALF - k], along[k])
    idle()

    def forward(yy, k, p):
        span = PIECES[p]
        send(part(0, yy, *span), part(2, yy, *span), fsend.at[1, k, p], frecv.at[1, k, p], beside)
        send(part(0, yy, *span), part(1, yy, *span), fsend.at[0, k, p], frecv.at[0, k, p], sibling)

    low, high = HALF - REACH, HALF + REACH + 1
    for p, span in enumerate(PIECES):
        if p == 0:
            for k in along:
                wait_for(single(HALF + k), zrecv.at[HALF + k])
            send(part(0, y, low, HALF), part(0, y, 0, low), zsend.at[2 * REACH], zrecv.at[0], along[REACH])
            send(
                part(0, y, HALF + 1, HALF + REACH),
                part(0, y, high, NZ),
                zsend.at[2 * REACH + 1],
                zrecv.at[high],
                along[-REACH],
            )
        else:
            wait_for(part(0, y, *span), zrecv.at[span[0]])
        for k in (2, 1, 3):
            send(part(0, y, *span), part(0, y, *span), ysend.at[k - 1, p], yrecv.at[k - 1, p], across[k - 1])
        forward(y, 0, p)
        for q in [p - 1] * (p > 0) + [p] * (p == len(PIECES) - 1):
            for k in (1, 3, 2):
                yy = (y + NY - k) % NY
                wait_for(part(0, yy, *PIECES[q]), yrecv.at[k - 1, q])
                forward(yy, k, q)
    for p, span in enumerate(PIECES):
        for k in range(NY):
            yy = (y + NY - k) % NY
            wait_for(part(1, yy, *span), frecv.at[0, k, p])
            wait_for(part(2, yy, *span), frecv.at[1, k, p])
    for copy in sends:
        copy.wait_send()


def gather_scratch():
    dma = pltpu.SemaphoreType.DMA
    parts = len(PIECES)
    return [
        dma((NZ,)),
        dma((NZ,)),
        dma((NY - 1, parts)),
        dma((NY - 1, parts)),
        dma((2, NY, parts)),
        dma((2, NY, parts)),
    ]


GATHER_SEMS = len(gather_scratch())


def spread(rows, refs):
    rows = list(rows) + [jnp.zeros((1, ATOMS), F32)] * (8 - len(rows))
    turned = jnp.transpose(jnp.concatenate(rows, axis=0))
    for f, ref in enumerate(refs):
        ref[...] = jnp.broadcast_to(turned[:, f : f + 1], (ATOMS, ATOMS))


def row_sums(values):
    ones = jnp.ones((8, ATOMS), jnp.bfloat16)
    total = jnp.zeros((8, ATOMS), F32)
    for step in range(3):
        part = values.astype(jnp.bfloat16)
        values = values - part.astype(F32)
        total = total + lax.dot_general(ones, part, NT, preferred_element_type=F32)
    return total[0:1]


def h_term(r2, a, ia8, s):
    ir = lax.rsqrt(r2)
    r = r2 * ir
    upper = r + s
    gap = s - r
    lower = jnp.maximum(a, jnp.abs(gap))
    il = 1.0 / lower
    iu = 1.0 / upper
    value = (il - iu) * (4.0 + (il + iu) * (s * s * ir - r)) + (ir + ir) * jnp.log(lower * iu)
    value = value + jnp.where(a < gap, ia8 - 8.0 * il, 0.0)
    return jnp.where(upper > a, value, 0.0)


def listed_codes(r, d, pairs, owners):
    odd = r % 2
    here = d // NY
    lane = lax.broadcasted_iota(I32, (1, ATOMS), 1)
    row = jnp.zeros((1, ATOMS), I32)
    for b in range(BLK):
        for k in range(SLOTS):
            cell = pairs[b, k]
            partner = owners[jnp.clip(cell, 0, NREG * REGION_BLOCKS - 1)]
            region = partner >> 8
            slot = jnp.where(region == r, 0, jnp.where(region == r + 1 - 2 * odd, 1, 2))
            offset = (((partner >> 4) & (NZ - 1)) - here + HALF) & (NZ - 1)
            place = slot * NDEV + ((partner >> 2) & (NY - 1)) * NZ + offset
            code = jnp.where(cell >= 0, place * BLK + (partner & (BLK - 1)) + 1, 0)
            row = jnp.where(lane == b * SLOTS + k, code, row)
    return row.astype(F32)


def merge_partners(r, forward, cells, known, found):
    previous = 2 - r % 2
    sub = lax.broadcasted_iota(I32, (16, ATOMS), 0)
    lane = lax.broadcasted_iota(I32, (16, ATOMS), 1)
    hits = jnp.zeros((16, ATOMS), F32)
    first = (sub & 3) * SLOTS
    for b in range(BLK):
        match = (known == cells[b]).astype(F32)
        pick = (((sub >> 2) == b) & (lane >= first) & (lane < first + SLOTS)).astype(F32)
        hits = hits + lax.dot_general(pick, match, NT, preferred_element_type=F32)
    start = (sub >> 2) * SLOTS
    listed = jnp.where((forward > 0.5) & (lane >= start) & (lane < start + SLOTS), 1.0, 0.0)
    row = lax.broadcasted_iota(I32, (ATOMS, ATOMS), 0)
    col = lax.broadcasted_iota(I32, (ATOMS, ATOMS), 1)
    prefix = (row <= col).astype(F32)
    ones = jnp.ones((ATOMS, ATOMS), F32)
    s0 = lax.broadcasted_iota(I32, (16, 16), 0)
    s1 = lax.broadcasted_iota(I32, (16, 16), 1)
    before = (((s0 >> 2) == (s1 >> 2)) & (s1 < s0)).astype(F32)
    earlier = jnp.dot(before, hits, preferred_element_type=F32) + listed
    rank = jnp.dot(hits, prefix, preferred_element_type=F32) + jnp.dot(earlier, ones, preferred_element_type=F32)
    rank = jnp.where(hits > 0.5, rank, 0.0)
    order = jnp.where(listed > 0.5, jnp.dot(listed, prefix, preferred_element_type=F32), 0.0)
    wanted = (lax.broadcasted_iota(I32, (REV, ATOMS), 0) + 1).astype(F32)
    place = lax.broadcasted_iota(I32, (1, ATOMS), 1)
    place = jnp.where(place < NDEV, place, place + (previous - 1) * NDEV)
    picked = []
    for b in range(BLK):
        total = jnp.where(order[b * BLK : b * BLK + 1] == wanted, forward, 0.0)
        for o in range(BLK):
            code = (place * BLK + o + 1).astype(F32)
            total = total + jnp.where(rank[b * BLK + o : b * BLK + o + 1] == wanted, code, 0.0)
        picked.append(total)
    picked = jnp.concatenate(picked, axis=0)
    codes = lax.dot_general(jnp.ones((8, ATOMS), F32), picked, NT, precision=HIGH, preferred_element_type=F32)
    found[...] = (codes + 0.5).astype(I32)


GROUP = 64


GROUP1 = 64
GROUP2 = 16
WIDE = 2


def groups(size=GROUP):
    return [pl.ds(g, size) for g in range(0, ATOMS, size)]


def diagonal(g):
    return lax.broadcasted_iota(I32, (GROUP, ATOMS), 1) == lax.broadcasted_iota(I32, (GROUP, ATOMS), 0) + g.start


def whole_kernel(
    pairs, owners_s, owners, pos, charges, types, out,
    x1, x2, fields, radii, home1, home2, acc1, acc2, geo, listed, found, found_s, local, *sems
):
    peers = far_peers()
    r, d, y, along, across, sibling, beside = peers
    everyone = list(along.values()) + across + [sibling, beside]
    barrier = pltpu.get_barrier_semaphore()
    for peer in everyone:
        pl.semaphore_signal(barrier, inc=1, device_id=peer, device_id_type=MESH)

    for b in range(BLK):
        for f in range(3):
            x1[0, 4 * f + b, :, :] = pos[f, b : b + 1, :]
        x1[0, 12 + b, :, :] = types[b : b + 1, :].astype(F32)
    lane = lax.broadcasted_iota(I32, (1, ATOMS), 1)
    row = jnp.full((1, ATOMS), -1, I32)
    for b in range(BLK):
        for k in range(SLOTS):
            row = jnp.where(lane == b * SLOTS + k, pairs[b, k], row)
    x1[0, 16, :, :] = row.astype(F32)
    ids = lax.broadcasted_iota(I32, (16, ATOMS), 0) * ATOMS + lax.broadcasted_iota(I32, (16, ATOMS), 1)
    held = owners[...]
    base = r * REGION_BLOCKS + d * BLK
    cells = [jnp.sum(jnp.where(held == base + b, ids, 0).astype(F32)) for b in range(BLK)]
    forward = listed_codes(r, d, pairs, owners_s)

    own_place = pl.ds(y * NZ + HALF, 1)

    def load_own(src, dst):
        copy = pltpu.make_async_copy(src, dst.at[own_place], local)
        copy.start()
        copy.wait()

    rho0 = table(types[...], type_radii)
    rho = rho0 - radius_offset
    scaled = table(types[...], type_scales) * rho

    def own_rows(b):
        return [pos[f, b : b + 1, :] for f in range(3)]

    def geometry(home, rows):
        dx, dy, dz = (h - v for h, v in zip(home, rows))
        return dx, dy, dz, dx * dx + dy * dy + dz * dz

    def own_descreen():
        for b in range(BLK):
            rho_b = rho[b : b + 1]
            spread(own_rows(b) + [rho_b, 8.0 / rho_b], [home1.at[b, f] for f in range(5)])
        for b in range(BLK):
            for g in groups():
                hx, hy, hz, ha, hi = (home1[b, f, g, :] for f in range(5))
                r2 = geometry((hx, hy, hz), own_rows(b))[3]
                mask = diagonal(g)
                acc1[b, g, :] = jnp.where(mask, 0.0, h_term(jnp.where(mask, 1.0, r2), ha, hi, scaled[b : b + 1]))

    load_own(x1, fields)
    pl.semaphore_wait(barrier, len(everyone))
    gather_body(peers, fields, *sems[:GATHER_SEMS], own_descreen)

    previous = 2 - r % 2
    for half, start in enumerate((0, previous * NDEV)):

        def take(n, carry, half=half, start=start):
            listed[pl.ds(half * NDEV + n, 1), :] = fields[start + n, 16]
            return carry

        lax.fori_loop(0, NDEV, take, 0, unroll=16)
    merge_partners(r, forward, cells, listed[...], found)
    copy = pltpu.make_async_copy(found, found_s, local)
    copy.start()
    copy.wait()

    def partner(b, n):
        code = found_s[0, b * REV + n]
        where = jnp.clip(code, 1, 3 * REGION_BLOCKS) - 1
        return code > 0, where >> 2, where & (BLK - 1)

    for b in range(BLK):

        def descreen_step(m, carry, b=b):
            sides = []
            for i in range(WIDE):
                live, place, block = partner(b, WIDE * m + i)
                rows = [fields[place, 4 * f + block] for f in range(3)]
                kind = fields[place, 12 + block]
                s = table(kind, scaled_values)
                sides.append((rows, jnp.where(live, s, NOWHERE)))
            for g in groups(GROUP1):
                hx, hy, hz, ha, hi = (home1[b, f, g, :] for f in range(5))
                terms = [h_term(geometry((hx, hy, hz), rows)[3], ha, hi, s) for rows, s in sides]
                acc1[b, g, :] += functools.reduce(jnp.add, terms)
            return carry

        lax.fori_loop(0, TILES // WIDE, descreen_step, 0)

    descreen = 0.125 * jnp.concatenate([row_sums(acc1[b]) for b in range(BLK)], axis=0)
    psi = descreen * rho
    shaped = born_alpha * psi - born_beta * psi * psi + born_gamma * psi * psi * psi
    born = 1.0 / (1.0 / rho - jnp.tanh(shaped) / rho0)
    out[0:4, :] = born
    for b in range(BLK):
        x2[0, b, :, :] = born[b : b + 1]
        x2[0, 4 + b, :, :] = charges[b : b + 1, :]
    load_own(x2, radii)

    inverse = 1.0 / born

    def energy_terms(geom, home, radius_j, inverse_j, charge_j, mask=None):
        dx, dy, dz, r2 = geom
        hq, hr, hd = home
        arg = r2 * (hd * inverse_j)
        damped = jnp.exp2(arg)
        inv = lax.rsqrt(r2 + hr * radius_j * damped)
        e = hq * charge_j * inv
        if mask is not None:
            e = jnp.where(mask, 0.0, e)
        e3 = e * (inv * inv)
        e3d = e3 * damped
        pull = e3 - 0.25 * e3d
        return pull * dx, pull * dy, pull * dz, e, (e3d * radius_j) * (1.0 - math.log(2.0) * arg)

    def while_radii_travel():
        for b in range(BLK):

            def geometry_step(n, carry, b=b):
                live, place, block = partner(b, n)
                rows = [fields[place, 4 * f + block] for f in range(3)]
                for g in groups():
                    geom = geometry([home1[b, f, g, :] for f in range(3)], rows)
                    for f in range(4):
                        geo[b * TILES + n, f, g, :] = geom[f]
                return carry

            lax.fori_loop(0, TILES, geometry_step, 0)
        for b in range(BLK):
            one = slice(b, b + 1)
            scale = (-0.25 * math.log2(math.e)) * inverse[one]
            spread([solvent_tau * charges[one, :], born[one], scale], [home2.at[b, f] for f in range(3)])
        for b in range(BLK):
            one = slice(b, b + 1)
            for g in groups():
                dx, dy, dz, r2 = geometry([home1[b, f, g, :] for f in range(3)], own_rows(b))
                mask = diagonal(g)
                geom = (dx, dy, dz, jnp.where(mask, 1.0, r2))
                home = [home2[b, f, g, :] for f in range(3)]
                terms = energy_terms(geom, home, born[one], inverse[one], charges[one, :], mask)
                for f in range(5):
                    acc2[b, f, g, :] = terms[f]

    gather_body(peers, radii, *sems[GATHER_SEMS:], while_radii_travel)

    for b in range(BLK):

        def energy_step(m, carry, b=b):
            sides = []
            for i in range(WIDE):
                live, place, block = partner(b, WIDE * m + i)
                radius_j = radii[place, block]
                charge_j = jnp.where(live, radii[place, 4 + block], 0.0)
                sides.append((b * TILES + WIDE * m + i, radius_j, 1.0 / radius_j, charge_j))
            for g in groups(GROUP2):
                home = [home2[b, f, g, :] for f in range(3)]
                terms = [energy_terms([geo[t, f, g, :] for f in range(4)], home, *rest) for t, *rest in sides]
                for f in range(5):
                    acc2[b, f, g, :] += functools.reduce(jnp.add, [term[f] for term in terms])
            return carry

        lax.fori_loop(0, TILES // WIDE, energy_step, 0)

    for b in range(BLK):
        one = slice(b, b + 1)
        for f in range(3):
            out[8 + 4 * f + b : 9 + 4 * f + b, :] = -row_sums(acc2[b, f])
        self_e = solvent_tau * charges[one, :] * charges[one, :]
        out[4 + b : 5 + b, :] = -0.5 * row_sums(acc2[b, 3]) - 0.5 * self_e * inverse[one]
        out[20 + b : 21 + b, :] = 0.5 * row_sums(acc2[b, 4]) + 0.5 * self_e * inverse[one] * inverse[one]


def whole(positions, charges, types, pairs, owner_map):
    smem = pl.BlockSpec(memory_space=pltpu.SMEM)
    vmem = pl.BlockSpec(memory_space=pltpu.VMEM)
    square = (ATOMS, ATOMS)
    return pl.pallas_call(
        whole_kernel,
        out_shape=jax.ShapeDtypeStruct((24, ATOMS), F32),
        in_specs=[smem, smem, vmem, vmem, vmem, vmem],
        out_specs=vmem,
        scratch_shapes=[
            pltpu.VMEM((1, ROWS1, 1, ATOMS), F32),
            pltpu.VMEM((1, ROWS2, 1, ATOMS), F32),
            pltpu.VMEM((3 * NDEV, ROWS1, 1, ATOMS), F32),
            pltpu.VMEM((3 * NDEV, ROWS2, 1, ATOMS), F32),
            pltpu.VMEM((BLK, 5) + square, F32),
            pltpu.VMEM((BLK, 3) + square, F32),
            pltpu.VMEM((BLK,) + square, F32),
            pltpu.VMEM((BLK, 5) + square, F32),
            pltpu.VMEM((BLK * TILES, 4) + square, F32),
            pltpu.VMEM(square, F32),
            pltpu.VMEM((8, ATOMS), I32),
            pltpu.SMEM((8, ATOMS), I32),
            pltpu.SemaphoreType.DMA,
        ]
        + gather_scratch()
        + gather_scratch(),
        compiler_params=pltpu.CompilerParams(
            collective_id=0, has_side_effects=True, vmem_limit_bytes=56 * 1024 * 1024
        ),
        name="whole",
    )(pairs, owner_map, owner_map.reshape(16, ATOMS), positions, charges, types)


def unpack_kernel(packed, born, energy, forces, grad):
    born[...] = packed[0:4, :]
    energy[...] = packed[4:8, :]
    for f in range(3):
        forces[f] = packed[8 + 4 * f : 12 + 4 * f, :]
    grad[...] = packed[20:24, :]


def shards(positions, charges, types, pairs, owner_map):
    packed = whole(positions, charges, types, pairs, owner_map)
    flat = jax.ShapeDtypeStruct((BLK, ATOMS), F32)
    vmem = pl.BlockSpec(memory_space=pltpu.VMEM)
    return pl.pallas_call(
        unpack_kernel,
        out_shape=(flat, flat, jax.ShapeDtypeStruct((3, BLK, ATOMS), F32), flat),
        in_specs=[vmem],
        out_specs=(vmem,) * 4,
        name="unpack",
    )(packed)


def solution(mesh):
    placed = (
        P(None, ("region", "dev"), None),
        P(("region", "dev"), None),
        P(("region", "dev"), None),
        P(("region", "dev"), None),
        P(),
    )
    return jax.shard_map(
        shards,
        mesh=mesh,
        in_specs=placed,
        out_specs=(
            P(("region", "dev"), None),
            P(("region", "dev"), None),
            P(None, ("region", "dev"), None),
            P(("region", "dev"), None),
        ),
        check_vma=False,
    )
```

```python
import functools
import math

import jax
import jax.numpy as jnp
import numpy as np
from jax import lax
from jax.experimental import pallas as pl
from jax.experimental.pallas import tpu as pltpu
from jax.sharding import PartitionSpec as P

type_radii = (1.2, 1.7, 1.55, 1.52, 1.85, 1.8)
type_scales = (0.85, 0.72, 0.79, 0.85, 0.86, 0.96)
radius_offset = 0.09
born_alpha = 1.0
born_beta = 0.8
born_gamma = 4.85
solvent_tau = 1.0 - 1.0 / 78.5

MESH = pl.DeviceIdType.MESH
NREG = 8
NZ = 16
NY = 4
NDEV = NZ * NY
BLK = 4
SLOTS = 13
ATOMS = 128
ROWS1 = 17
ROWS2 = 8
REGION_BLOCKS = NDEV * BLK
REV = 32
LIST = 64
HALF = NZ // 2
REACH = 4
PIECES = ((4, 13), (0, 4), (13, 16))
ORDER = ((0,), (0, (1, 3)), (1,), (2,), (0, (2,)), (1, (1, 3, 2)), (2, (1, 3, 2)))
DIRECT1 = (False, True, True)
DIRECT2 = (False, True, True)
F32 = jnp.float32
I32 = jnp.int32
NT = (((1,), (1,)), ((), ()))


scaled_values = [float(np.float32(s) * (np.float32(v) - np.float32(radius_offset))) for s, v in zip(type_scales, type_radii)]


def table(types, values):
    out = jnp.full(types.shape, values[0], F32)
    for i in range(1, len(values)):
        out = jnp.where(types == i, F32(values[i]), out)
    return out


TILES = 2 * SLOTS
NOWHERE = -1e30


def far_peers():
    r = lax.axis_index("region")
    d = lax.axis_index("dev")
    z = d // NY
    y = d % NY
    odd = r % 2
    hops = sorted((k for k in range(-REACH, REACH + 1) if k), key=abs)
    along = {k: (r, (z + k + NZ) % NZ * NY + y) for k in hops}
    across = [(r, z * NY + (y + k) % NY) for k in range(1, NY)]
    sibling = (r + 1 - 2 * odd, d)
    other = (r + 2 * odd - 1 + NREG) % NREG
    beside = [(other, z * NY + (y + k) % NY) for k in range(NY)]
    return r, d, y, along, across, sibling, beside


def gather_body(peers, direct, out, zsend, zrecv, ysend, yrecv, fsend, frecv, idle):
    r, d, y, along, across, sibling, beside = peers
    sends = []

    def send(src, dst, ssem, rsem, to):
        copy = pltpu.make_async_remote_copy(
            src_ref=src, dst_ref=dst, send_sem=ssem, recv_sem=rsem, device_id=to, device_id_type=MESH
        )
        copy.start()
        sends.append(copy)

    def wait_for(dst, rsem):
        pltpu.make_async_remote_copy(
            src_ref=dst, dst_ref=dst, send_sem=rsem, recv_sem=rsem, device_id=sibling, device_id_type=MESH
        ).wait_recv()

    def part(slot, yy, a, b):
        return out.at[pl.ds((slot * NY + yy) * NZ + a, b - a)]

    def single(o):
        return part(0, y, o, o + 1)

    for n, k in enumerate(along):
        send(single(HALF), single(HALF - k), zsend.at[n], zrecv.at[HALF - k], along[k])
    idle()

    def forward(yy, k, p):
        span = PIECES[p]
        if not direct[p]:
            send(part(0, yy, *span), part(2, yy, *span), fsend.at[1, k, p], frecv.at[1, k, p], beside[0])
        send(part(0, yy, *span), part(1, yy, *span), fsend.at[0, k, p], frecv.at[0, k, p], sibling)

    low, high = HALF - REACH, HALF + REACH + 1

    def along_done(p):
        span = PIECES[p]
        if p == 0:
            for k in along:
                wait_for(single(HALF + k), zrecv.at[HALF + k])
            send(part(0, y, low, HALF), part(0, y, 0, low), zsend.at[2 * REACH], zrecv.at[0], along[REACH])
            send(
                part(0, y, HALF + 1, HALF + REACH),
                part(0, y, high, NZ),
                zsend.at[2 * REACH + 1],
                zrecv.at[high],
                along[-REACH],
            )
        else:
            wait_for(part(0, y, *span), zrecv.at[span[0]])
        for k in (2, 1, 3):
            send(part(0, y, *span), part(0, y, *span), ysend.at[k - 1, p], yrecv.at[k - 1, p], across[k - 1])
        for k in (2, 1, 3, 0) if direct[p] else ():
            send(part(0, y, *span), part(2, y, *span), fsend.at[1, k, p], frecv.at[1, k, p], beside[k])
        forward(y, 0, p)

    def across_done(p, ks):
        for k in ks:
            yy = (y + NY - k) % NY
            wait_for(part(0, yy, *PIECES[p]), yrecv.at[k - 1, p])
            forward(yy, k, p)

    for leg in ORDER:
        if len(leg) == 1:
            along_done(*leg)
        else:
            across_done(*leg)
    for p, span in enumerate(PIECES):
        for k in range(NY):
            yy = (y + NY - k) % NY
            wait_for(part(1, yy, *span), frecv.at[0, k, p])
            wait_for(part(2, yy, *span), frecv.at[1, k, p])
    for copy in sends:
        copy.wait_send()


def gather_scratch():
    dma = pltpu.SemaphoreType.DMA
    parts = len(PIECES)
    return [
        dma((NZ,)),
        dma((NZ,)),
        dma((NY - 1, parts)),
        dma((NY - 1, parts)),
        dma((2, NY, parts)),
        dma((2, NY, parts)),
    ]


GATHER_SEMS = len(gather_scratch())


def spread(rows, refs):
    rows = list(rows) + [jnp.zeros((1, ATOMS), F32)] * (8 - len(rows))
    turned = jnp.transpose(jnp.concatenate(rows, axis=0))
    for f, ref in enumerate(refs):
        ref[...] = jnp.broadcast_to(turned[:, f : f + 1], (ATOMS, ATOMS))


def row_sums(values):
    eye = lax.broadcasted_iota(I32, values.shape, 0) == lax.broadcasted_iota(I32, values.shape, 1)
    return jnp.sum(jnp.where(eye, jnp.sum(values, axis=1, keepdims=True), 0.0), axis=0, keepdims=True)


def h_term(r2, a, ia8, s):
    ir = lax.rsqrt(r2)
    r = r2 * ir
    upper = r + s
    gap = s - r
    lower = jnp.maximum(a, jnp.abs(gap))
    il = 1.0 / lower
    iu = 1.0 / upper
    value = (il - iu) * (4.0 + (il + iu) * (s * s * ir - r)) + ((2.0 * math.log(2.0)) * ir) * lax.log2(lower * iu)
    value = value + jnp.where(a < gap, ia8 - 8.0 * il, 0.0)
    return jnp.where(upper > a, value, 0.0)


def listed_codes(r, d, pairs, owners):
    odd = r % 2
    here = d // NY
    lane = lax.broadcasted_iota(I32, (1, ATOMS), 1)
    row = jnp.zeros((1, ATOMS), I32)
    for b in range(BLK):
        for k in range(SLOTS):
            cell = pairs[b, k]
            partner = owners[jnp.clip(cell, 0, NREG * REGION_BLOCKS - 1)]
            region = partner >> 8
            slot = jnp.where(region == r, 0, jnp.where(region == r + 1 - 2 * odd, 1, 2))
            offset = (((partner >> 4) & (NZ - 1)) - here + HALF) & (NZ - 1)
            place = slot * NDEV + ((partner >> 2) & (NY - 1)) * NZ + offset
            code = jnp.where(cell >= 0, place * BLK + (partner & (BLK - 1)) + 1, 0)
            row = jnp.where(lane == b * SLOTS + k, code, row)
    return row.astype(F32)


def merge_partners(r, forward, cells, known, found):
    previous = 2 - r % 2
    sub = lax.broadcasted_iota(I32, (16, ATOMS), 0)
    lane = lax.broadcasted_iota(I32, (16, ATOMS), 1)
    hits = jnp.zeros((16, ATOMS), F32)
    first = (sub & 3) * SLOTS
    for b in range(BLK):
        match = (known == cells[b]).astype(F32)
        pick = (((sub >> 2) == b) & (lane >= first) & (lane < first + SLOTS)).astype(F32)
        hits = hits + lax.dot_general(pick, match, NT, preferred_element_type=F32)
    start = (sub >> 2) * SLOTS
    listed = jnp.where((forward > 0.5) & (lane >= start) & (lane < start + SLOTS), 1.0, 0.0)
    row = lax.broadcasted_iota(I32, (ATOMS, ATOMS), 0)
    col = lax.broadcasted_iota(I32, (ATOMS, ATOMS), 1)
    prefix = (row <= col).astype(F32)
    ones = jnp.ones((ATOMS, ATOMS), F32)
    s0 = lax.broadcasted_iota(I32, (16, 16), 0)
    s1 = lax.broadcasted_iota(I32, (16, 16), 1)
    before = (((s0 >> 2) == (s1 >> 2)) & (s1 < s0)).astype(F32)
    earlier = jnp.dot(before, hits, preferred_element_type=F32) + listed
    rank = jnp.dot(hits, prefix, preferred_element_type=F32) + jnp.dot(earlier, ones, preferred_element_type=F32)
    rank = jnp.where(hits > 0.5, rank, 0.0)
    order = jnp.where(listed > 0.5, jnp.dot(listed, prefix, preferred_element_type=F32), 0.0)
    wanted = (lax.broadcasted_iota(I32, (REV, ATOMS), 0) + 1).astype(F32)
    place = lax.broadcasted_iota(I32, (1, ATOMS), 1)
    place = jnp.where(place < NDEV, place, place + (previous - 1) * NDEV)
    picked = []
    for b in range(BLK):
        total = jnp.where(order[b * BLK : b * BLK + 1] == wanted, forward, 0.0)
        for o in range(BLK):
            code = (place * BLK + o + 1).astype(F32)
            total = total + jnp.where(rank[b * BLK + o : b * BLK + o + 1] == wanted, code, 0.0)
        picked.append(total)
    picked = jnp.concatenate(picked, axis=0)
    found[...] = jnp.broadcast_to((row_sums(picked) + 0.5).astype(I32), found.shape)


GROUP = 64


GROUP1 = 64
GROUP2 = 16
WIDE = 2


def groups(size=GROUP):
    return [pl.ds(g, size) for g in range(0, ATOMS, size)]


def diagonal(g):
    return lax.broadcasted_iota(I32, (GROUP, ATOMS), 1) == lax.broadcasted_iota(I32, (GROUP, ATOMS), 0) + g.start


def whole_kernel(
    pairs_in, owners_s_in, owners_in, pos_in, charges_in, types_in, out,
    pairs, owners_s, owners, pos, charges, types, brought, x1, x2, fields, radii, home1, home2, acc1, acc2, geo, listed, found, found_s, local, *sems
):
    targets = (pairs, owners_s, owners, pos, charges, types)
    sources = (pairs_in, owners_s_in, owners_in, pos_in, charges_in, types_in)
    inputs = [pltpu.make_async_copy(src, dst, brought.at[i]) for i, (src, dst) in enumerate(zip(sources, targets))]
    for copy in inputs:
        copy.start()
    peers = far_peers()
    r, d, y, along, across, sibling, beside = peers
    everyone = list(along.values()) + across + [sibling] + beside
    barrier = pltpu.get_barrier_semaphore()
    for peer in everyone:
        pl.semaphore_signal(barrier, inc=1, device_id=peer, device_id_type=MESH)

    for copy in inputs:
        copy.wait()

    for b in range(BLK):
        for f in range(3):
            x1[0, 4 * f + b, :, :] = pos[f, b : b + 1, :]
        x1[0, 12 + b, :, :] = types[b : b + 1, :].astype(F32)
    lane = lax.broadcasted_iota(I32, (1, ATOMS), 1)
    row = jnp.full((1, ATOMS), -1, I32)
    for b in range(BLK):
        for k in range(SLOTS):
            row = jnp.where(lane == b * SLOTS + k, pairs[b, k], row)
    x1[0, 16, :, :] = row.astype(F32)
    own_place = pl.ds(y * NZ + HALF, 1)

    def load_own(src, dst):
        copy = pltpu.make_async_copy(src, dst.at[own_place], local)
        copy.start()
        copy.wait()

    rho0 = table(types[...], type_radii)
    rho = rho0 - radius_offset
    scaled = table(types[...], type_scales) * rho

    forward = cells = None

    def own_rows(b):
        return [pos[f, b : b + 1, :] for f in range(3)]

    def geometry(home, rows):
        dx, dy, dz = (h - v for h, v in zip(home, rows))
        return dx, dy, dz, dx * dx + dy * dy + dz * dz

    def own_descreen():
        nonlocal forward, cells
        ids = lax.broadcasted_iota(I32, (16, ATOMS), 0) * ATOMS + lax.broadcasted_iota(I32, (16, ATOMS), 1)
        held = owners[...]
        base = r * REGION_BLOCKS + d * BLK
        cells = [jnp.sum(jnp.where(held == base + b, ids, 0).astype(F32)) for b in range(BLK)]
        forward = listed_codes(r, d, pairs, owners_s)
        for b in range(BLK):
            rho_b = rho[b : b + 1]
            spread(own_rows(b) + [rho_b, 8.0 / rho_b], [home1.at[b, f] for f in range(5)])
        for b in range(BLK):
            for g in groups():
                hx, hy, hz, ha, hi = (home1[b, f, g, :] for f in range(5))
                r2 = geometry((hx, hy, hz), own_rows(b))[3]
                mask = diagonal(g)
                acc1[b, g, :] = jnp.where(mask, 0.0, h_term(jnp.where(mask, 1.0, r2), ha, hi, scaled[b : b + 1]))

    load_own(x1, fields)
    pl.semaphore_wait(barrier, len(everyone))
    gather_body(peers, DIRECT1, fields, *sems[:GATHER_SEMS], own_descreen)

    previous = 2 - r % 2
    for half, start in enumerate((0, previous * NDEV)):

        def take(n, carry, half=half, start=start):
            listed[pl.ds(half * NDEV + n, 1), :] = fields[start + n, 16]
            return carry

        lax.fori_loop(0, NDEV, take, 0, unroll=16)
    merge_partners(r, forward, cells, listed[...], found)
    copy = pltpu.make_async_copy(found, found_s, local)
    copy.start()
    copy.wait()

    def partner(b, n):
        code = found_s[0, b * REV + n]
        where = jnp.clip(code, 1, 3 * REGION_BLOCKS) - 1
        return code > 0, where >> 2, where & (BLK - 1)

    for b in range(BLK):

        def descreen_step(m, carry, b=b):
            sides = []
            for i in range(WIDE):
                live, place, block = partner(b, WIDE * m + i)
                rows = [fields[place, 4 * f + block] for f in range(3)]
                kind = fields[place, 12 + block]
                s = table(kind, scaled_values)
                sides.append((rows, jnp.where(live, s, NOWHERE)))
            for g in groups(GROUP1):
                hx, hy, hz, ha, hi = (home1[b, f, g, :] for f in range(5))
                terms = [h_term(geometry((hx, hy, hz), rows)[3], ha, hi, s) for rows, s in sides]
                acc1[b, g, :] += functools.reduce(jnp.add, terms)
            return carry

        lax.fori_loop(0, TILES // WIDE, descreen_step, 0)

    descreen = 0.125 * jnp.concatenate([row_sums(acc1[b]) for b in range(BLK)], axis=0)
    psi = descreen * rho
    shaped = born_alpha * psi - born_beta * psi * psi + born_gamma * psi * psi * psi
    born = 1.0 / (1.0 / rho - jnp.tanh(shaped) / rho0)
    out[0:4, :] = born
    for b in range(BLK):
        x2[0, b, :, :] = born[b : b + 1]
        x2[0, 4 + b, :, :] = charges[b : b + 1, :]
    load_own(x2, radii)

    inverse = 1.0 / born

    def energy_terms(geom, home, radius_j, inverse_j, charge_j, mask=None):
        dx, dy, dz, r2 = geom
        hq, hr, hd = home
        arg = r2 * (hd * inverse_j)
        damped = jnp.exp2(arg)
        inv = lax.rsqrt(r2 + hr * radius_j * damped)
        e = hq * charge_j * inv
        if mask is not None:
            e = jnp.where(mask, 0.0, e)
        e3 = e * (inv * inv)
        e3d = e3 * damped
        pull = e3 - 0.25 * e3d
        return pull * dx, pull * dy, pull * dz, e, (e3d * radius_j) * (1.0 - math.log(2.0) * arg)

    def while_radii_travel():
        for b in range(BLK):

            def geometry_step(n, carry, b=b):
                live, place, block = partner(b, n)
                rows = [fields[place, 4 * f + block] for f in range(3)]
                for g in groups():
                    geom = geometry([home1[b, f, g, :] for f in range(3)], rows)
                    for f in range(4):
                        geo[b * TILES + n, f, g, :] = geom[f]
                return carry

            lax.fori_loop(0, TILES, geometry_step, 0)
        for b in range(BLK):
            one = slice(b, b + 1)
            scale = (-0.25 * math.log2(math.e)) * inverse[one]
            spread([solvent_tau * charges[one, :], born[one], scale], [home2.at[b, f] for f in range(3)])
        for b in range(BLK):
            one = slice(b, b + 1)
            for g in groups():
                dx, dy, dz, r2 = geometry([home1[b, f, g, :] for f in range(3)], own_rows(b))
                mask = diagonal(g)
                geom = (dx, dy, dz, jnp.where(mask, 1.0, r2))
                home = [home2[b, f, g, :] for f in range(3)]
                terms = energy_terms(geom, home, born[one], inverse[one], charges[one, :], mask)
                for f in range(5):
                    acc2[b, f, g, :] = terms[f]

    gather_body(peers, DIRECT2, radii, *sems[GATHER_SEMS:], while_radii_travel)

    for b in range(BLK):

        def energy_step(m, carry, b=b):
            sides = []
            for i in range(WIDE):
                live, place, block = partner(b, WIDE * m + i)
                radius_j = radii[place, block]
                charge_j = jnp.where(live, radii[place, 4 + block], 0.0)
                sides.append((b * TILES + WIDE * m + i, radius_j, 1.0 / radius_j, charge_j))
            for g in groups(GROUP2):
                home = [home2[b, f, g, :] for f in range(3)]
                terms = [energy_terms([geo[t, f, g, :] for f in range(4)], home, *rest) for t, *rest in sides]
                for f in range(5):
                    acc2[b, f, g, :] += functools.reduce(jnp.add, [term[f] for term in terms])
            return carry

        lax.fori_loop(0, TILES // WIDE, energy_step, 0)

    for b in range(BLK):
        one = slice(b, b + 1)
        for f in range(3):
            out[8 + 4 * f + b : 9 + 4 * f + b, :] = -row_sums(acc2[b, f])
        self_e = solvent_tau * charges[one, :] * charges[one, :]
        out[4 + b : 5 + b, :] = -0.5 * row_sums(acc2[b, 3]) - 0.5 * self_e * inverse[one]
        out[20 + b : 21 + b, :] = 0.5 * row_sums(acc2[b, 4]) + 0.5 * self_e * inverse[one] * inverse[one]


def whole(positions, charges, types, pairs, owner_map):
    vmem = pl.BlockSpec(memory_space=pltpu.VMEM)
    square = (ATOMS, ATOMS)
    return pl.pallas_call(
        whole_kernel,
        out_shape=jax.ShapeDtypeStruct((24, ATOMS), F32),
        in_specs=[pl.BlockSpec(memory_space=pl.ANY)] * 6,
        out_specs=vmem,
        scratch_shapes=[
            pltpu.SMEM((BLK, SLOTS), I32),
            pltpu.SMEM((NREG * REGION_BLOCKS,), I32),
            pltpu.VMEM((16, ATOMS), I32),
            pltpu.VMEM((3, BLK, ATOMS), F32),
            pltpu.VMEM((BLK, ATOMS), F32),
            pltpu.VMEM((BLK, ATOMS), I32),
            pltpu.SemaphoreType.DMA((6,)),
            pltpu.VMEM((1, ROWS1, 1, ATOMS), F32),
            pltpu.VMEM((1, ROWS2, 1, ATOMS), F32),
            pltpu.VMEM((3 * NDEV, ROWS1, 1, ATOMS), F32),
            pltpu.VMEM((3 * NDEV, ROWS2, 1, ATOMS), F32),
            pltpu.VMEM((BLK, 5) + square, F32),
            pltpu.VMEM((BLK, 3) + square, F32),
            pltpu.VMEM((BLK,) + square, F32),
            pltpu.VMEM((BLK, 5) + square, F32),
            pltpu.VMEM((BLK * TILES, 4) + square, F32),
            pltpu.VMEM(square, F32),
            pltpu.VMEM((8, ATOMS), I32),
            pltpu.SMEM((8, ATOMS), I32),
            pltpu.SemaphoreType.DMA,
        ]
        + gather_scratch()
        + gather_scratch(),
        compiler_params=pltpu.CompilerParams(
            collective_id=0, has_side_effects=True, vmem_limit_bytes=56 * 1024 * 1024
        ),
        name="whole",
    )(pairs, owner_map, owner_map.reshape(16, ATOMS), positions, charges, types)


def unpack_kernel(packed, born, energy, forces, grad):
    born[...] = packed[0:4, :]
    energy[...] = packed[4:8, :]
    for f in range(3):
        forces[f] = packed[8 + 4 * f : 12 + 4 * f, :]
    grad[...] = packed[20:24, :]


def shards(positions, charges, types, pairs, owner_map):
    packed = whole(positions, charges, types, pairs, owner_map)
    flat = jax.ShapeDtypeStruct((BLK, ATOMS), F32)
    vmem = pl.BlockSpec(memory_space=pltpu.VMEM)
    return pl.pallas_call(
        unpack_kernel,
        out_shape=(flat, flat, jax.ShapeDtypeStruct((3, BLK, ATOMS), F32), flat),
        in_specs=[vmem],
        out_specs=(vmem,) * 4,
        name="unpack",
    )(packed)


def solution(mesh):
    placed = (
        P(None, ("region", "dev"), None),
        P(("region", "dev"), None),
        P(("region", "dev"), None),
        P(("region", "dev"), None),
        P(),
    )
    return jax.shard_map(
        shards,
        mesh=mesh,
        in_specs=placed,
        out_specs=(
            P(("region", "dev"), None),
            P(("region", "dev"), None),
            P(None, ("region", "dev"), None),
            P(("region", "dev"), None),
        ),
        check_vma=False,
    )
```

```python
import functools
import math

import jax
import jax.numpy as jnp
import numpy as np
from jax import lax
from jax.experimental import pallas as pl
from jax.experimental.pallas import tpu as pltpu
from jax.sharding import PartitionSpec as P

type_radii = (1.2, 1.7, 1.55, 1.52, 1.85, 1.8)
type_scales = (0.85, 0.72, 0.79, 0.85, 0.86, 0.96)
radius_offset = 0.09
born_alpha = 1.0
born_beta = 0.8
born_gamma = 4.85
solvent_tau = 1.0 - 1.0 / 78.5

MESH = pl.DeviceIdType.MESH
NREG = 8
NZ = 16
NY = 4
NDEV = NZ * NY
BLK = 4
SLOTS = 13
ATOMS = 128
ROWS1 = 17
ROWS2 = 8
REGION_BLOCKS = NDEV * BLK
REV = 32
LIST = 64
HALF = NZ // 2
REACH = 4
PIECES = ((4, 13), (0, 4), (13, 16))
ORDER = ((0,), (0, (1, 3)), (1,), (2,), (0, (2,)), (1, (1, 3, 2)), (2, (1, 3, 2)))
DIRECT1 = (False, True, True)
DIRECT2 = (False, True, True)
F32 = jnp.float32
I32 = jnp.int32
NT = (((1,), (1,)), ((), ()))


scaled_values = [float(np.float32(s) * (np.float32(v) - np.float32(radius_offset))) for s, v in zip(type_scales, type_radii)]


def table(types, values):
    out = jnp.full(types.shape, values[0], F32)
    for i in range(1, len(values)):
        out = jnp.where(types == i, F32(values[i]), out)
    return out


TILES = 2 * SLOTS
NOWHERE = -1e30


def far_peers():
    r = lax.axis_index("region")
    d = lax.axis_index("dev")
    z = d // NY
    y = d % NY
    odd = r % 2
    hops = sorted((k for k in range(-REACH, REACH + 1) if k), key=abs)
    along = {k: (r, (z + k + NZ) % NZ * NY + y) for k in hops}
    across = [(r, z * NY + (y + k) % NY) for k in range(1, NY)]
    sibling = (r + 1 - 2 * odd, d)
    other = (r + 2 * odd - 1 + NREG) % NREG
    beside = [(other, z * NY + (y + k) % NY) for k in range(NY)]
    return r, d, y, along, across, sibling, beside


def gather_body(peers, direct, out, zsend, zrecv, ysend, yrecv, fsend, frecv, idle):
    r, d, y, along, across, sibling, beside = peers
    sends = []

    def send(src, dst, ssem, rsem, to):
        copy = pltpu.make_async_remote_copy(
            src_ref=src, dst_ref=dst, send_sem=ssem, recv_sem=rsem, device_id=to, device_id_type=MESH
        )
        copy.start()
        sends.append(copy)

    def wait_for(dst, rsem):
        pltpu.make_async_remote_copy(
            src_ref=dst, dst_ref=dst, send_sem=rsem, recv_sem=rsem, device_id=sibling, device_id_type=MESH
        ).wait_recv()

    def part(slot, yy, a, b):
        return out.at[pl.ds((slot * NY + yy) * NZ + a, b - a)]

    def single(o):
        return part(0, y, o, o + 1)

    for n, k in enumerate(along):
        send(single(HALF), single(HALF - k), zsend.at[n], zrecv.at[HALF - k], along[k])
    idle()

    def forward(yy, k, p):
        span = PIECES[p]
        if not direct[p]:
            send(part(0, yy, *span), part(2, yy, *span), fsend.at[1, k, p], frecv.at[1, k, p], beside[0])
        send(part(0, yy, *span), part(1, yy, *span), fsend.at[0, k, p], frecv.at[0, k, p], sibling)

    low, high = HALF - REACH, HALF + REACH + 1

    def along_done(p):
        span = PIECES[p]
        if p == 0:
            for k in along:
                wait_for(single(HALF + k), zrecv.at[HALF + k])
            send(part(0, y, low, HALF), part(0, y, 0, low), zsend.at[2 * REACH], zrecv.at[0], along[REACH])
            send(
                part(0, y, HALF + 1, HALF + REACH),
                part(0, y, high, NZ),
                zsend.at[2 * REACH + 1],
                zrecv.at[high],
                along[-REACH],
            )
        else:
            wait_for(part(0, y, *span), zrecv.at[span[0]])
        for k in (2, 1, 3):
            send(part(0, y, *span), part(0, y, *span), ysend.at[k - 1, p], yrecv.at[k - 1, p], across[k - 1])
        for k in (2, 1, 3, 0) if direct[p] else ():
            send(part(0, y, *span), part(2, y, *span), fsend.at[1, k, p], frecv.at[1, k, p], beside[k])
        forward(y, 0, p)

    def across_done(p, ks):
        for k in ks:
            yy = (y + NY - k) % NY
            wait_for(part(0, yy, *PIECES[p]), yrecv.at[k - 1, p])
            forward(yy, k, p)

    for leg in ORDER:
        if len(leg) == 1:
            along_done(*leg)
        else:
            across_done(*leg)
    for p, span in enumerate(PIECES):
        for k in range(NY):
            yy = (y + NY - k) % NY
            wait_for(part(1, yy, *span), frecv.at[0, k, p])
            wait_for(part(2, yy, *span), frecv.at[1, k, p])
    for copy in sends:
        copy.wait_send()


def gather_scratch():
    dma = pltpu.SemaphoreType.DMA
    parts = len(PIECES)
    return [
        dma((2 * REACH + 2,)),
        dma((HALF + REACH + 2,)),
        dma((NY - 1, parts)),
        dma((NY - 1, parts)),
        dma((2, NY, parts)),
        dma((2, NY, parts)),
    ]


GATHER_SEMS = len(gather_scratch())


def spread(rows, refs):
    rows = list(rows) + [jnp.zeros((1, ATOMS), F32)] * (8 - len(rows))
    turned = jnp.transpose(jnp.concatenate(rows, axis=0))
    for f, ref in enumerate(refs):
        ref[...] = jnp.broadcast_to(turned[:, f : f + 1], (ATOMS, ATOMS))


def row_sums(values):
    eye = lax.broadcasted_iota(I32, values.shape, 0) == lax.broadcasted_iota(I32, values.shape, 1)
    return jnp.sum(jnp.where(eye, jnp.sum(values, axis=1, keepdims=True), 0.0), axis=0, keepdims=True)


def h_term(r2, a, ia8, s):
    ir = lax.rsqrt(r2)
    r = r2 * ir
    upper = r + s
    gap = s - r
    lower = jnp.maximum(a, jnp.abs(gap))
    il = 1.0 / lower
    iu = 1.0 / upper
    value = (il - iu) * (4.0 + (il + iu) * (s * s * ir - r)) + ((2.0 * math.log(2.0)) * ir) * lax.log2(lower * iu)
    value = value + jnp.where(a < gap, ia8 - 8.0 * il, 0.0)
    return jnp.where(upper > a, value, 0.0)


def listed_codes(r, d, pairs, owners):
    odd = r % 2
    here = d // NY
    lane = lax.broadcasted_iota(I32, (1, ATOMS), 1)
    row = jnp.zeros((1, ATOMS), I32)
    for b in range(BLK):
        for k in range(SLOTS):
            cell = pairs[b, k]
            partner = owners[jnp.clip(cell, 0, NREG * REGION_BLOCKS - 1)]
            region = partner >> 8
            slot = jnp.where(region == r, 0, jnp.where(region == r + 1 - 2 * odd, 1, 2))
            offset = (((partner >> 4) & (NZ - 1)) - here + HALF) & (NZ - 1)
            place = slot * NDEV + ((partner >> 2) & (NY - 1)) * NZ + offset
            code = jnp.where(cell >= 0, place * BLK + (partner & (BLK - 1)) + 1, 0)
            row = jnp.where(lane == b * SLOTS + k, code, row)
    return row.astype(F32)


def merge_partners(r, forward, cells, known, found):
    previous = 2 - r % 2
    sub = lax.broadcasted_iota(I32, (16, ATOMS), 0)
    lane = lax.broadcasted_iota(I32, (16, ATOMS), 1)
    hits = jnp.zeros((16, ATOMS), F32)
    first = (sub & 3) * SLOTS
    for b in range(BLK):
        match = (known == cells[b]).astype(F32)
        pick = (((sub >> 2) == b) & (lane >= first) & (lane < first + SLOTS)).astype(F32)
        hits = hits + lax.dot_general(pick, match, NT, preferred_element_type=F32)
    start = (sub >> 2) * SLOTS
    listed = jnp.where((forward > 0.5) & (lane >= start) & (lane < start + SLOTS), 1.0, 0.0)
    row = lax.broadcasted_iota(I32, (ATOMS, ATOMS), 0)
    col = lax.broadcasted_iota(I32, (ATOMS, ATOMS), 1)
    prefix = (row <= col).astype(F32)
    ones = jnp.ones((ATOMS, ATOMS), F32)
    s0 = lax.broadcasted_iota(I32, (16, 16), 0)
    s1 = lax.broadcasted_iota(I32, (16, 16), 1)
    before = (((s0 >> 2) == (s1 >> 2)) & (s1 < s0)).astype(F32)
    earlier = jnp.dot(before, hits, preferred_element_type=F32) + listed
    rank = jnp.dot(hits, prefix, preferred_element_type=F32) + jnp.dot(earlier, ones, preferred_element_type=F32)
    rank = jnp.where(hits > 0.5, rank, 0.0)
    order = jnp.where(listed > 0.5, jnp.dot(listed, prefix, preferred_element_type=F32), 0.0)
    wanted = (lax.broadcasted_iota(I32, (REV, ATOMS), 0) + 1).astype(F32)
    place = lax.broadcasted_iota(I32, (1, ATOMS), 1)
    place = jnp.where(place < NDEV, place, place + (previous - 1) * NDEV)
    picked = []
    for b in range(BLK):
        total = jnp.where(order[b * BLK : b * BLK + 1] == wanted, forward, 0.0)
        for o in range(BLK):
            code = (place * BLK + o + 1).astype(F32)
            total = total + jnp.where(rank[b * BLK + o : b * BLK + o + 1] == wanted, code, 0.0)
        picked.append(total)
    picked = jnp.concatenate(picked, axis=0)
    codes = (row_sums(picked) + 0.5).astype(I32)
    for b in range(BLK):
        for n in range(TILES):
            found[b, n] = codes[0, b * REV + n]


GROUP = 64


GROUP1 = 64
GROUP2 = 16
WIDE = 2


def groups(size=GROUP):
    return [pl.ds(g, size) for g in range(0, ATOMS, size)]


def diagonal(g):
    return lax.broadcasted_iota(I32, (GROUP, ATOMS), 1) == lax.broadcasted_iota(I32, (GROUP, ATOMS), 0) + g.start


def whole_kernel(
    pairs_in, owners_s_in, owners_in, pos_in, charges_in, types_in, out,
    pairs, owners_s, owners, pos, charges, types, brought, x1, x2, fields, radii, home1, home2, acc1, acc2, geo, listed, found, local, *sems
):
    targets = (pairs, owners_s, owners, pos, charges, types)
    sources = (pairs_in, owners_s_in, owners_in, pos_in, charges_in, types_in)
    inputs = [pltpu.make_async_copy(src, dst, brought.at[i]) for i, (src, dst) in enumerate(zip(sources, targets))]
    for copy in inputs:
        copy.start()
    peers = far_peers()
    r, d, y, along, across, sibling, beside = peers
    everyone = list(along.values()) + across + [sibling] + beside
    barrier = pltpu.get_barrier_semaphore()
    for peer in everyone:
        pl.semaphore_signal(barrier, inc=1, device_id=peer, device_id_type=MESH)

    for copy in inputs:
        copy.wait()

    for b in range(BLK):
        for f in range(3):
            x1[0, 4 * f + b, :, :] = pos[f, b : b + 1, :]
        x1[0, 12 + b, :, :] = types[b : b + 1, :].astype(F32)
    lane = lax.broadcasted_iota(I32, (1, ATOMS), 1)
    row = jnp.full((1, ATOMS), -1, I32)
    for b in range(BLK):
        for k in range(SLOTS):
            row = jnp.where(lane == b * SLOTS + k, pairs[b, k], row)
    x1[0, 16, :, :] = row.astype(F32)
    own_place = pl.ds(y * NZ + HALF, 1)

    def load_own(src, dst):
        copy = pltpu.make_async_copy(src, dst.at[own_place], local)
        copy.start()
        copy.wait()

    rho0 = table(types[...], type_radii)
    rho = rho0 - radius_offset
    scaled = table(types[...], type_scales) * rho

    forward = cells = None

    def own_rows(b):
        return [pos[f, b : b + 1, :] for f in range(3)]

    def geometry(home, rows):
        dx, dy, dz = (h - v for h, v in zip(home, rows))
        return dx, dy, dz, dx * dx + dy * dy + dz * dz

    def own_descreen():
        nonlocal forward, cells
        ids = lax.broadcasted_iota(I32, (16, ATOMS), 0) * ATOMS + lax.broadcasted_iota(I32, (16, ATOMS), 1)
        held = owners[...]
        base = r * REGION_BLOCKS + d * BLK
        cells = [jnp.sum(jnp.where(held == base + b, ids, 0).astype(F32)) for b in range(BLK)]
        forward = listed_codes(r, d, pairs, owners_s)
        for b in range(BLK):
            rho_b = rho[b : b + 1]
            spread(own_rows(b) + [rho_b, 8.0 / rho_b], [home1.at[b, f] for f in range(5)])
        for b in range(BLK):
            for g in groups():
                hx, hy, hz, ha, hi = (home1[b, f, g, :] for f in range(5))
                r2 = geometry((hx, hy, hz), own_rows(b))[3]
                mask = diagonal(g)
                acc1[b, g, :] = jnp.where(mask, 0.0, h_term(jnp.where(mask, 1.0, r2), ha, hi, scaled[b : b + 1]))

    load_own(x1, fields)
    pl.semaphore_wait(barrier, len(everyone))
    first = sems[:GATHER_SEMS]
    again = [sem for pair in zip(first[::2], sems[GATHER_SEMS:]) for sem in pair]
    gather_body(peers, DIRECT1, fields, *first, own_descreen)

    previous = 2 - r % 2
    for half, start in enumerate((0, previous * NDEV)):

        def take(n, carry, half=half, start=start):
            listed[pl.ds(half * NDEV + n, 1), :] = fields[start + n, 16]
            return carry

        lax.fori_loop(0, NDEV, take, 0, unroll=16)
    merge_partners(r, forward, cells, listed[...], found)

    def partner(b, n):
        code = found[b, n]
        where = jnp.clip(code, 1, 3 * REGION_BLOCKS) - 1
        return code > 0, where >> 2, where & (BLK - 1)

    for b in range(BLK):

        def descreen_step(m, carry, b=b):
            sides = []
            for i in range(WIDE):
                live, place, block = partner(b, WIDE * m + i)
                rows = [fields[place, 4 * f + block] for f in range(3)]
                kind = fields[place, 12 + block]
                s = table(kind, scaled_values)
                sides.append((rows, jnp.where(live, s, NOWHERE)))
            for g in groups(GROUP1):
                hx, hy, hz, ha, hi = (home1[b, f, g, :] for f in range(5))
                terms = [h_term(geometry((hx, hy, hz), rows)[3], ha, hi, s) for rows, s in sides]
                acc1[b, g, :] += functools.reduce(jnp.add, terms)
            return carry

        lax.fori_loop(0, TILES // WIDE, descreen_step, 0)

    descreen = 0.125 * jnp.concatenate([row_sums(acc1[b]) for b in range(BLK)], axis=0)
    psi = descreen * rho
    shaped = born_alpha * psi - born_beta * psi * psi + born_gamma * psi * psi * psi
    born = 1.0 / (1.0 / rho - jnp.tanh(shaped) / rho0)
    out[0:4, :] = born
    for b in range(BLK):
        x2[0, b, :, :] = born[b : b + 1]
        x2[0, 4 + b, :, :] = charges[b : b + 1, :]
    load_own(x2, radii)

    inverse = 1.0 / born

    def energy_terms(geom, home, radius_j, inverse_j, charge_j, mask=None):
        dx, dy, dz, r2 = geom
        hq, hr, hd = home
        arg = r2 * (hd * inverse_j)
        damped = jnp.exp2(arg)
        inv = lax.rsqrt(r2 + hr * radius_j * damped)
        e = hq * charge_j * inv
        if mask is not None:
            e = jnp.where(mask, 0.0, e)
        e3 = e * (inv * inv)
        e3d = e3 * damped
        pull = e3 - 0.25 * e3d
        return pull * dx, pull * dy, pull * dz, e, (e3d * radius_j) * (1.0 - math.log(2.0) * arg)

    def while_radii_travel():
        for b in range(BLK):

            def geometry_step(n, carry, b=b):
                live, place, block = partner(b, n)
                rows = [fields[place, 4 * f + block] for f in range(3)]
                for g in groups():
                    geom = geometry([home1[b, f, g, :] for f in range(3)], rows)
                    for f in range(4):
                        geo[b * TILES + n, f, g, :] = geom[f]
                return carry

            lax.fori_loop(0, TILES, geometry_step, 0)
        for b in range(BLK):
            one = slice(b, b + 1)
            scale = (-0.25 * math.log2(math.e)) * inverse[one]
            spread([solvent_tau * charges[one, :], born[one], scale], [home2.at[b, f] for f in range(3)])
        for b in range(BLK):
            one = slice(b, b + 1)
            for g in groups():
                dx, dy, dz, r2 = geometry([home1[b, f, g, :] for f in range(3)], own_rows(b))
                mask = diagonal(g)
                geom = (dx, dy, dz, jnp.where(mask, 1.0, r2))
                home = [home2[b, f, g, :] for f in range(3)]
                terms = energy_terms(geom, home, born[one], inverse[one], charges[one, :], mask)
                for f in range(5):
                    acc2[b, f, g, :] = terms[f]

    gather_body(peers, DIRECT2, radii, *again, while_radii_travel)

    for b in range(BLK):

        def energy_step(m, carry, b=b):
            sides = []
            for i in range(WIDE):
                live, place, block = partner(b, WIDE * m + i)
                radius_j = radii[place, block]
                charge_j = jnp.where(live, radii[place, 4 + block], 0.0)
                sides.append((b * TILES + WIDE * m + i, radius_j, 1.0 / radius_j, charge_j))
            for g in groups(GROUP2):
                home = [home2[b, f, g, :] for f in range(3)]
                terms = [energy_terms([geo[t, f, g, :] for f in range(4)], home, *rest) for t, *rest in sides]
                for f in range(5):
                    acc2[b, f, g, :] += functools.reduce(jnp.add, [term[f] for term in terms])
            return carry

        lax.fori_loop(0, TILES // WIDE, energy_step, 0)

    for b in range(BLK):
        one = slice(b, b + 1)
        for f in range(3):
            out[8 + 4 * f + b : 9 + 4 * f + b, :] = -row_sums(acc2[b, f])
        self_e = solvent_tau * charges[one, :] * charges[one, :]
        out[4 + b : 5 + b, :] = -0.5 * row_sums(acc2[b, 3]) - 0.5 * self_e * inverse[one]
        out[20 + b : 21 + b, :] = 0.5 * row_sums(acc2[b, 4]) + 0.5 * self_e * inverse[one] * inverse[one]


def whole(positions, charges, types, pairs, owner_map):
    vmem = pl.BlockSpec(memory_space=pltpu.VMEM)
    square = (ATOMS, ATOMS)
    return pl.pallas_call(
        whole_kernel,
        out_shape=jax.ShapeDtypeStruct((24, ATOMS), F32),
        in_specs=[pl.BlockSpec(memory_space=pl.ANY)] * 6,
        out_specs=vmem,
        scratch_shapes=[
            pltpu.SMEM((BLK, SLOTS), I32),
            pltpu.SMEM((NREG * REGION_BLOCKS,), I32),
            pltpu.VMEM((16, ATOMS), I32),
            pltpu.VMEM((3, BLK, ATOMS), F32),
            pltpu.VMEM((BLK, ATOMS), F32),
            pltpu.VMEM((BLK, ATOMS), I32),
            pltpu.SemaphoreType.DMA((6,)),
            pltpu.VMEM((1, ROWS1, 1, ATOMS), F32),
            pltpu.VMEM((1, ROWS2, 1, ATOMS), F32),
            pltpu.VMEM((3 * NDEV, ROWS1, 1, ATOMS), F32),
            pltpu.VMEM((3 * NDEV, ROWS2, 1, ATOMS), F32),
            pltpu.VMEM((BLK, 5) + square, F32),
            pltpu.VMEM((BLK, 3) + square, F32),
            pltpu.VMEM((BLK,) + square, F32),
            pltpu.VMEM((BLK, 5) + square, F32),
            pltpu.VMEM((BLK * TILES, 4) + square, F32),
            pltpu.VMEM(square, F32),
            pltpu.SMEM((BLK, TILES), I32),
            pltpu.SemaphoreType.DMA,
        ]
        + gather_scratch()
        + gather_scratch()[1::2],
        compiler_params=pltpu.CompilerParams(
            collective_id=0, has_side_effects=True, vmem_limit_bytes=56 * 1024 * 1024
        ),
        name="whole",
    )(pairs, owner_map, owner_map.reshape(16, ATOMS), positions, charges, types)


def unpack_kernel(packed, born, energy, forces, grad):
    born[...] = packed[0:4, :]
    energy[...] = packed[4:8, :]
    for f in range(3):
        forces[f] = packed[8 + 4 * f : 12 + 4 * f, :]
    grad[...] = packed[20:24, :]


def shards(positions, charges, types, pairs, owner_map):
    packed = whole(positions, charges, types, pairs, owner_map)
    flat = jax.ShapeDtypeStruct((BLK, ATOMS), F32)
    vmem = pl.BlockSpec(memory_space=pltpu.VMEM)
    return pl.pallas_call(
        unpack_kernel,
        out_shape=(flat, flat, jax.ShapeDtypeStruct((3, BLK, ATOMS), F32), flat),
        in_specs=[vmem],
        out_specs=(vmem,) * 4,
        name="unpack",
    )(packed)


def solution(mesh):
    placed = (
        P(None, ("region", "dev"), None),
        P(("region", "dev"), None),
        P(("region", "dev"), None),
        P(("region", "dev"), None),
        P(),
    )
    return jax.shard_map(
        shards,
        mesh=mesh,
        in_specs=placed,
        out_specs=(
            P(("region", "dev"), None),
            P(("region", "dev"), None),
            P(None, ("region", "dev"), None),
            P(("region", "dev"), None),
        ),
        check_vma=False,
    )
```
